32 devices in a mesh: seq: 8 (over z, x), dp: 4 (over y, core).
Axes of the slice: x: 2, y: 2, z: 4, core: 2. Of those that a mesh axis runs over, the one named last changes fastest.
Arguments:
- inputs: float32 [4, 2048, 768], P('dp', 'seq'), may hold values from -6 to 6
- doc_ids: int32 [4, 2048], P('dp'), may hold values from 0 to 1, as said below
- cotangent: float32 [4, 2048, 768], P('dp', 'seq'), may hold values from -6 to 6
- ln1_gain: bfloat16 [768], P(('seq', 'dp')), may hold values from 0.099609375 to 1.8984375
- ln1_shift: bfloat16 [768], P(('seq', 'dp')), may hold values from -3 to 3
- w_qkv: bfloat16 [768, 2304], P(('seq', 'dp')), may hold values from -0.21875 to 0.21875
- b_query: bfloat16 [768], P(('seq', 'dp')), may hold values from -3 to 3
- b_value: bfloat16 [768], P(('seq', 'dp')), may hold values from -3 to 3
- w_attn_out: bfloat16 [768, 768], P(('seq', 'dp')), may hold values from -1.75 to 1.75
- b_attn_out: bfloat16 [768], P(('seq', 'dp')), may hold values from -3 to 3
- ln2_gain: bfloat16 [768], P(('seq', 'dp')), may hold values from 0.099609375 to 1.8984375
- ln2_shift: bfloat16 [768], P(('seq', 'dp')), may hold values from -3 to 3
- w_fc: bfloat16 [768, 3072], P(('seq', 'dp')), may hold values from -0.21875 to 0.21875
- b_fc: bfloat16 [3072], P(('seq', 'dp')), may hold values from -3 to 3
- w_mlp_out: bfloat16 [3072, 768], P(('seq', 'dp')), may hold values from -0.109375 to 0.109375
- b_mlp_out: bfloat16 [768], P(('seq', 'dp')), may hold values from -3 to 3
Outputs:
- result: float32 [4, 2048, 768], P('dp', 'seq')
- grad_inputs: float32 [4, 2048, 768], P('dp', 'seq')
- grad_ln1_gain: float32 [768], P(('seq', 'dp'))
- grad_ln1_shift: float32 [768], P(('seq', 'dp'))
- grad_w_qkv: float32 [768, 2304], P(('seq', 'dp'))
- grad_b_query: float32 [768], P(('seq', 'dp'))
- grad_b_value: float32 [768], P(('seq', 'dp'))
- grad_w_attn_out: float32 [768, 768], P(('seq', 'dp'))
- grad_b_attn_out: float32 [768], P(('seq', 'dp'))
- grad_ln2_gain: float32 [768], P(('seq', 'dp'))
- grad_ln2_shift: float32 [768], P(('seq', 'dp'))
- grad_w_fc: float32 [768, 3072], P(('seq', 'dp'))
- grad_b_fc: float32 [3072], P(('seq', 'dp'))
- grad_w_mlp_out: float32 [3072, 768], P(('seq', 'dp'))
- grad_b_mlp_out: float32 [768], P(('seq', 'dp'))
The draws below stay inside these ranges and needn't reach their ends.
Inputs may be any that keep to these rules, and one draw needn't show every extreme that they name: `doc_ids`: within each group, document numbers never fall and start at 0. Every group holds two documents: one of exactly 1792 tokens and one of 256 tokens, in either order, so the boundary falls at 256 or at 1792.
All inputs are finite; a program needn't handle non-finite values.
Results may differ from the reference program's by a relative error of at most 0.019.
Values may be sent and summed in bfloat16 or wider, within the bound.
No kernel may reach another device: no remote copies, remote signals or barrier semaphores. Data moves between devices by JAX's collectives and lax.ppermute only.
A program may use at most 192 MiB of HBM per device.

```python
import jax
import jax.numpy as jnp
from jax import lax

D = 768
FF = 3072
HEADS = 12
HEAD_DIM = 64
TOK_DEV = 256
GROUPS = 4
GROUP_TOK = 2048
LONG = 1792


def draw_doc_ids(key, part):
    start_key = jax.random.fold_in(key, 11)
    first_block = jax.random.randint(start_key, (GROUPS, 1), 0, 2).astype(jnp.int32)
    positions = jnp.arange(GROUP_TOK, dtype=jnp.int32)
    boundary = jnp.where(first_block == 0, LONG, TOK_DEV).astype(jnp.int32)
    return (positions[None, :] >= boundary).astype(jnp.int32)


def block_levels(stream_key, extent, shards, smallest, largest):
    def one(position, blocks):
        steps = jax.random.uniform(jax.random.fold_in(jax.random.fold_in(stream_key, 6), position), (blocks,), jnp.float32, smallest / len(shards), largest / len(shards))
        return jnp.repeat(jnp.exp(steps), extent[position] // blocks).reshape((-1,) + (1,) * (len(extent) - position - 1))

    level = one(*shards[0])
    for cut in shards[1:]:
        level = level * one(*cut)
    return level


def gaussian(own_key, dims, width, limit, cuts=(), kind=jnp.bfloat16):
    entries = jax.random.normal(own_key, dims, jnp.float32) * width
    if len(cuts) > 0:
        entries = block_levels(own_key, dims, cuts, -0.22, 0.18) * entries
    return jnp.clip(entries, min=-limit, max=limit).astype(kind)


def setup_inputs(seed: int = 0) -> dict:
    key_list = jax.random.split(jax.random.key(seed), 17)
    return {
        "inputs": gaussian(key_list[0], (GROUPS, GROUP_TOK, D), 1.0, 6.0, ((0, 4), (1, 8)), jnp.float32),
        "doc_ids": draw_doc_ids(jax.random.fold_in(key_list[16], 71), 0),
        "cotangent": gaussian(key_list[2], (GROUPS, GROUP_TOK, D), 1.0, 6.0, ((0, 4), (1, 8)), jnp.float32),
        "ln1_gain": jnp.clip(1.0 + 0.18 * jax.random.normal(key_list[3], (D,), jnp.float32), 0.099609375, 1.8984375).astype(jnp.bfloat16),
        "ln1_shift": gaussian(key_list[4], (D,), 0.5, 3.0, ((0, 32),)),
        "w_qkv": gaussian(key_list[5], (D, 3 * D), D ** -0.5, 0.21875, ((0, 32),)),
        "b_query": gaussian(key_list[6], (D,), 0.5, 3.0, ((0, 32),)),
        "b_value": gaussian(key_list[7], (D,), 0.5, 3.0, ((0, 32),)),
        "w_attn_out": gaussian(key_list[8], (D, D), (D // 64) ** -0.5, 1.75, ((0, 32),)),
        "b_attn_out": gaussian(key_list[9], (D,), 0.5, 3.0, ((0, 32),)),
        "ln2_gain": jnp.clip(1.0 + 0.18 * jax.random.normal(key_list[10], (D,), jnp.float32), 0.099609375, 1.8984375).astype(jnp.bfloat16),
        "ln2_shift": gaussian(key_list[11], (D,), 0.5, 3.0, ((0, 32),)),
        "w_fc": gaussian(key_list[12], (D, FF), D ** -0.5, 0.21875, ((0, 32),)),
        "b_fc": gaussian(key_list[13], (FF,), 0.5, 3.0, ((0, 32),)),
        "w_mlp_out": gaussian(key_list[14], (FF, D), FF ** -0.5, 0.109375, ((0, 32),)),
        "b_mlp_out": gaussian(key_list[15], (D,), 0.5, 3.0, ((0, 32),)),
    }


norm_eps = 1e-05
gelu_root = 0.7978845608028654
gelu_cube = 0.044715
score_scale = 0.125

def layer_norm(values, gain, shift):
    average = lax.optimization_barrier(jnp.mean(values, axis=-1, keepdims=True))
    centred = values - average
    variance = lax.optimization_barrier(jnp.mean(centred * centred, axis=-1, keepdims=True))
    inverse = lax.rsqrt(variance + norm_eps)
    normed = centred * inverse
    return (normed * gain.astype(jnp.float32) + shift.astype(jnp.float32), normed, inverse)

def norm_back(grad_out, normed, inverse, gain):
    scaled = grad_out * gain.astype(jnp.float32)
    first = lax.optimization_barrier(jnp.mean(scaled, axis=-1, keepdims=True))
    second = lax.optimization_barrier(jnp.mean(scaled * normed, axis=-1, keepdims=True))
    return inverse * (scaled - first - normed * second)

def gelu_pair(values):
    inner = gelu_root * (values + gelu_cube * values * values * values)
    tangent = jnp.tanh(inner)
    output = 0.5 * values * (1.0 + tangent)
    slope = 0.5 * (1.0 + tangent) + 0.5 * values * (1.0 - tangent * tangent) * gelu_root * (1.0 + 3.0 * gelu_cube * values * values)
    return (output, slope)

def group_pass(params, tokens, group_docs, grad_out):
    gain_one, shift_one, qkv_full, query_bias, value_bias, proj_full, proj_bias, gain_two, shift_two, fc_full, fc_bias, out_full, out_bias = params
    length = tokens.shape[0]
    positions = jnp.arange(length, dtype=jnp.int32)
    visible = (group_docs[:, None] == group_docs[None, :]) & (positions[None, :] <= positions[:, None])
    normed_in, normal_one, inverse_one = layer_norm(tokens, gain_one, shift_one)
    attn_in = normed_in.astype(jnp.bfloat16)
    qkv_bias = jnp.concatenate([query_bias.astype(jnp.float32), jnp.zeros((D,), jnp.float32), value_bias.astype(jnp.float32)])
    qkv_rows = jnp.dot(attn_in, qkv_full, preferred_element_type=jnp.float32) + qkv_bias
    qkv_bf = qkv_rows.astype(jnp.bfloat16)

    def split_heads(block):
        return block.reshape(length, HEADS, HEAD_DIM).transpose(1, 0, 2)
    queries = split_heads(qkv_bf[:, :D])
    keys = split_heads(qkv_bf[:, D:2 * D])
    values = split_heads(qkv_bf[:, 2 * D:])

    def head_forward(items):
        query, key, value = items
        scores = jnp.dot(query, key.T, preferred_element_type=jnp.float32) * score_scale
        masked = jnp.where(visible, scores, -1e+30)
        top = lax.optimization_barrier(jnp.max(masked, axis=-1))
        total = lax.optimization_barrier(jnp.sum(jnp.where(visible, jnp.exp(masked - top[:, None]), 0.0), axis=-1))
        lse = top + jnp.log(total)
        probs = jnp.where(visible, jnp.exp(scores - lse[:, None]), 0.0).astype(jnp.bfloat16)
        return (jnp.dot(probs, value, preferred_element_type=jnp.float32), lse)
    head_out, lse_all = lax.map(head_forward, (queries, keys, values))
    attended = head_out.transpose(1, 0, 2).reshape(length, D)
    attended_bf = attended.astype(jnp.bfloat16)
    resid_one = tokens + jnp.dot(attended_bf, proj_full, preferred_element_type=jnp.float32) + proj_bias.astype(jnp.float32)
    normed_mid, normal_two, inverse_two = layer_norm(resid_one, gain_two, shift_two)
    mlp_in = normed_mid.astype(jnp.bfloat16)
    hidden_pre = jnp.dot(mlp_in, fc_full, preferred_element_type=jnp.float32) + fc_bias.astype(jnp.float32)
    hidden_act, hidden_slope = gelu_pair(hidden_pre)
    hidden_bf = hidden_act.astype(jnp.bfloat16)
    result = resid_one + jnp.dot(hidden_bf, out_full, preferred_element_type=jnp.float32) + out_bias.astype(jnp.float32)
    grad_bf = grad_out.astype(jnp.bfloat16)
    g_out_w = jnp.dot(hidden_bf.T, grad_bf, preferred_element_type=jnp.float32)
    g_out_b = lax.optimization_barrier(jnp.sum(grad_out, axis=0))
    grad_hidden = jnp.dot(grad_bf, out_full.T, preferred_element_type=jnp.float32) * hidden_slope
    hidden_grad_bf = grad_hidden.astype(jnp.bfloat16)
    g_fc_w = jnp.dot(mlp_in.T, hidden_grad_bf, preferred_element_type=jnp.float32)
    g_fc_b = lax.optimization_barrier(jnp.sum(grad_hidden, axis=0))
    grad_mid = jnp.dot(hidden_grad_bf, fc_full.T, preferred_element_type=jnp.float32)
    g_gain_two = lax.optimization_barrier(jnp.sum(grad_mid * normal_two, axis=0))
    g_shift_two = lax.optimization_barrier(jnp.sum(grad_mid, axis=0))
    grad_resid = grad_out + norm_back(grad_mid, normal_two, inverse_two, gain_two)
    resid_bf = grad_resid.astype(jnp.bfloat16)
    g_proj_w = jnp.dot(attended_bf.T, resid_bf, preferred_element_type=jnp.float32)
    g_proj_b = lax.optimization_barrier(jnp.sum(grad_resid, axis=0))
    grad_attn = jnp.dot(resid_bf, proj_full.T, preferred_element_type=jnp.float32)
    grad_heads = grad_attn.reshape(length, HEADS, HEAD_DIM).transpose(1, 0, 2)
    delta_all = lax.optimization_barrier(jnp.sum(grad_heads * head_out, axis=-1))
    grad_heads_bf = grad_heads.astype(jnp.bfloat16)

    def head_backward(items):
        query, key, value, grad_head, lse, delta = items
        scores = jnp.dot(query, key.T, preferred_element_type=jnp.float32) * score_scale
        prob_full = jnp.where(visible, jnp.exp(scores - lse[:, None]), 0.0)
        probs = prob_full.astype(jnp.bfloat16)
        grad_value = jnp.dot(probs.T, grad_head, preferred_element_type=jnp.float32)
        grad_prob = jnp.dot(grad_head, value.T, preferred_element_type=jnp.float32)
        grad_score = (prob_full * (grad_prob - delta[:, None])).astype(jnp.bfloat16)
        grad_query = score_scale * jnp.dot(grad_score, key, preferred_element_type=jnp.float32)
        grad_key = score_scale * jnp.dot(grad_score.T, query, preferred_element_type=jnp.float32)
        return (grad_query, grad_key, grad_value)
    grad_q, grad_k, grad_v = lax.map(head_backward, (queries, keys, values, grad_heads_bf, lse_all, delta_all))

    def merge_heads(block):
        return block.transpose(1, 0, 2).reshape(length, D)
    grad_q = merge_heads(grad_q)
    grad_k = merge_heads(grad_k)
    grad_v = merge_heads(grad_v)
    qkv_grad_bf = jnp.concatenate([grad_q, grad_k, grad_v], axis=1).astype(jnp.bfloat16)
    g_qkv_w = jnp.dot(attn_in.T, qkv_grad_bf, preferred_element_type=jnp.float32)
    g_query_b = lax.optimization_barrier(jnp.sum(grad_q, axis=0))
    g_value_b = lax.optimization_barrier(jnp.sum(grad_v, axis=0))
    grad_first = jnp.dot(qkv_grad_bf, qkv_full.T, preferred_element_type=jnp.float32)
    g_gain_one = lax.optimization_barrier(jnp.sum(grad_first * normal_one, axis=0))
    g_shift_one = lax.optimization_barrier(jnp.sum(grad_first, axis=0))
    grad_input = grad_resid + norm_back(grad_first, normal_one, inverse_one, gain_one)
    terms = (g_gain_one, g_shift_one, g_qkv_w, g_query_b, g_value_b, g_proj_w, g_proj_b, g_gain_two, g_shift_two, g_fc_w, g_fc_b, g_out_w, g_out_b)
    return (result, grad_input, terms)

def reference(inputs, doc_ids, cotangent, ln1_gain, ln1_shift, w_qkv, b_query, b_value, w_attn_out, b_attn_out, ln2_gain, ln2_shift, w_fc, b_fc, w_mlp_out, b_mlp_out):
    params = (ln1_gain, ln1_shift, w_qkv, b_query, b_value, w_attn_out, b_attn_out, ln2_gain, ln2_shift, w_fc, b_fc, w_mlp_out, b_mlp_out)
    starts = tuple((jnp.zeros(param.shape, jnp.float32) for param in params))

    def group_step(totals, data):
        tokens, group_docs, grad_out = data
        result, grad_input, terms = group_pass(params, tokens, group_docs, grad_out)
        return (tuple((first + second for first, second in zip(totals, terms))), (result, grad_input))
    totals, outputs = lax.scan(group_step, starts, (inputs, doc_ids, cotangent))
    result, grad_input = outputs
    return (result, grad_input, totals[0], totals[1], totals[2], totals[3], totals[4], totals[5], totals[6], totals[7], totals[8], totals[9], totals[10], totals[11], totals[12])
```

```python
import functools

import jax
import jax.numpy as jnp
from jax import lax
from jax.experimental import pallas as pl
from jax.experimental.pallas import tpu as pltpu
from jax.sharding import PartitionSpec as P

HEADS = 12
LANES = 128

norm_eps = 1e-05
gelu_root = 0.7978845608028654
gelu_cube = 0.044715
score_scale = 0.125
hidden_score = -1e30


bf16 = jnp.bfloat16
f32 = jnp.float32


def layer_norm(values, gain, shift):
    average = jnp.mean(values, axis=-1, keepdims=True)
    centred = values - average
    variance = jnp.mean(centred * centred, axis=-1, keepdims=True)
    inverse = lax.rsqrt(variance + norm_eps)
    normed = centred * inverse
    return (normed * gain + shift, normed, inverse)


def norm_back(grad_out, normed, inverse, gain):
    scaled = grad_out * gain
    first = jnp.mean(scaled, axis=-1, keepdims=True)
    second = jnp.mean(scaled * normed, axis=-1, keepdims=True)
    return inverse * (scaled - first - normed * second)


def gelu_pair(values):
    inner = gelu_root * (values + gelu_cube * values * values * values)
    tangent = jnp.tanh(inner)
    output = 0.5 * values * (1.0 + tangent)
    slope = 0.5 * (1.0 + tangent) + 0.5 * values * (1.0 - tangent * tangent) * gelu_root * (
        1.0 + 3.0 * gelu_cube * values * values
    )
    return (output, slope)


def dot(left, right, left_dim, right_dim):
    return lax.dot_general(
        left, right, (((left_dim,), (right_dim,)), ((), ())), preferred_element_type=f32
    )


def bits_of(sizes):
    out = []
    for axis in ("seq", "dp"):
        bit = sizes[axis] // 2
        while bit >= 1:
            out.append((axis, bit))
            bit //= 2
    return out


def step_orders(sizes):
    order = bits_of(sizes)
    seq_bits = [s for s in order if s[0] == "seq"]
    dp_bits = [s for s in order if s[0] == "dp"]
    far, near = seq_bits[:-1], seq_bits[-1:]
    side, core = dp_bits[:-1], dp_bits[-1:]
    return (far + near + side + core, far + side + near + core)


def own_bit(step):
    axis, bit = step
    return (lax.axis_index(axis) // bit) % 2 == 1


def exchange(value, step, sizes):
    axis, bit = step
    return lax.ppermute(value, axis, [(i, i ^ bit) for i in range(sizes[axis])])


def gather(shard, steps, sizes):
    place = {step: n for n, step in enumerate(bits_of(sizes))}
    have, value = [], shard
    for step in steps:
        other = exchange(value, step, sizes)
        at = sum(1 for n in have if n < place[step])
        upper = own_bit(step)
        low = jnp.where(upper, other, value)
        high = jnp.where(upper, value, other)
        value = jnp.stack([low, high], axis=at)
        have.append(place[step])
    return value.reshape((-1,) + shard.shape[1:])


def scatter_sum(full, steps, sizes, kind):
    order = bits_of(sizes)
    count = 2 ** len(order)
    value = full.reshape((2,) * len(order) + (full.shape[0] // count,) + full.shape[1:])
    left = list(order)
    for step in reversed(steps):
        at = left.index(step)
        low = lax.index_in_dim(value, 0, at, keepdims=False)
        high = lax.index_in_dim(value, 1, at, keepdims=False)
        upper = own_bit(step)
        keep = jnp.where(upper, high, low)
        send = jnp.where(upper, low, high)
        got = exchange(send.astype(kind), step, sizes)
        left.remove(step)
        value = keep.astype(f32) + got.astype(f32)
        if left:
            value = value.astype(kind)
    return value


def block_slot(far_pos, index, far):
    return lax.rem(far_pos - index + far, far)


def triangle(size):
    key_pos = lax.broadcasted_iota(jnp.int32, (size, size), 0)
    query_pos = lax.broadcasted_iota(jnp.int32, (size, size), 1)
    return jnp.where(key_pos <= query_pos, 0.0, hidden_score)


def forward_kernel(heads, dim, far, where_ref, own_ref, pair_ref, out_ref, out_bf_ref, lse_ref, tri_ref):
    far_pos, near_pos = where_ref[0], where_ref[1]
    rows = heads * dim
    tri_ref[...] = triangle(tri_ref.shape[0])

    def head_rows(part, head):
        return pl.ds(part * rows + head * dim, dim)

    def query_block(j, _):
        first = where_ref[2 + j]
        slot_j = block_slot(far_pos, j, far)
        queries = [
            own_ref[slot_j, head_rows(0, h), :] * jnp.asarray(score_scale, bf16)
            for h in range(heads)
        ]

        def tiles(i, state, diagonal):
            slot_i = block_slot(far_pos, i, far)
            own_at, pair_at = 2 * i + near_pos, 2 * i + 1 - near_pos
            own_bias = jnp.where(own_at >= first, 0.0, hidden_score)
            pair_seen = (pair_at >= first) & (pair_at < 2 * j + near_pos)
            pair_bias = jnp.where(pair_seen, 0.0, hidden_score)
            out = []
            for h in range(heads):
                top, total, acc = state[h]
                own = dot(own_ref[slot_i, head_rows(1, h), :], queries[h], 0, 0)
                own = own + (tri_ref[...] if diagonal else own_bias)
                pair = dot(pair_ref[slot_i, head_rows(0, h), :], queries[h], 0, 0) + pair_bias
                new_top = jnp.maximum(top, jnp.max(jnp.maximum(own, pair), axis=0, keepdims=True))
                own = jnp.exp(own - new_top)
                pair = jnp.exp(pair - new_top)
                shrink = jnp.exp(top - new_top)
                total = total * shrink + jnp.sum(own + pair, axis=0, keepdims=True)
                acc = (
                    acc * shrink
                    + dot(own_ref[slot_i, head_rows(2, h), :], own.astype(bf16), 1, 0)
                    + dot(pair_ref[slot_i, head_rows(1, h), :], pair.astype(bf16), 1, 0)
                )
                out.append((new_top, total, acc))
            return tuple(out)

        size = own_ref.shape[2]
        state = tuple(
            (
                jnp.full((1, size), hidden_score, f32),
                jnp.zeros((1, size), f32),
                jnp.zeros((dim, size), f32),
            )
            for _ in range(heads)
        )
        state = lax.fori_loop(first // 2, j, lambda i, s: tiles(i, s, False), state)
        state = tiles(j, state, True)
        for h in range(heads):
            top, total, acc = state[h]
            done = acc / total
            out_ref[slot_j, pl.ds(h * dim, dim), :] = done
            out_bf_ref[slot_j, pl.ds(h * dim, dim), :] = done.astype(bf16)
            lse_ref[slot_j, pl.ds(h, 1), :] = top + jnp.log(total)
        return 0

    lax.fori_loop(0, far, query_block, 0)


def backward_kernel(
    heads, dim, far,
    where_ref, own_ref, pair_ref, grad_ref, out_ref, lse_ref,
    query_ref, own_grad_ref, pair_grad_ref, tri_ref, acc_ref,
):
    far_pos, near_pos = where_ref[0], where_ref[1]
    rows = heads * dim
    tri_ref[...] = triangle(tri_ref.shape[0])
    own_grad_ref[...] = jnp.zeros(own_grad_ref.shape, f32)
    acc_ref[...] = jnp.zeros(acc_ref.shape, f32)

    def head_rows(part, head):
        return pl.ds(part * rows + head * dim, dim)

    def query_block(j, _):
        first = where_ref[2 + j]
        slot_j = block_slot(far_pos, j, far)
        queries = [
            own_ref[slot_j, head_rows(0, h), :] * jnp.asarray(score_scale, bf16)
            for h in range(heads)
        ]
        grads = [grad_ref[slot_j, head_rows(0, h), :] for h in range(heads)]
        deltas = [
            jnp.sum(grads[h].astype(f32) * out_ref[slot_j, head_rows(0, h), :], axis=0, keepdims=True)
            for h in range(heads)
        ]
        lses = [lse_ref[slot_j, pl.ds(h, 1), :] for h in range(heads)]

        def tile(h, keys, vals, bias, into, slot_i):
            scores = dot(keys, queries[h], 0, 0)
            prob = jnp.exp(scores + bias - lses[h])
            grad_prob = dot(vals, grads[h], 0, 0)
            grad_score = (prob * (grad_prob - deltas[h])).astype(bf16)
            into[slot_i, head_rows(0, h), :] += dot(queries[h], grad_score, 1, 1)
            into[slot_i, head_rows(1, h), :] += dot(grads[h], prob.astype(bf16), 1, 1)
            return dot(keys, grad_score, 1, 0)

        def tiles(i, state, diagonal):
            slot_i = block_slot(far_pos, i, far)
            own_at, pair_at = 2 * i + near_pos, 2 * i + 1 - near_pos
            own_bias = jnp.where(own_at >= first, 0.0, hidden_score)
            pair_seen = (pair_at >= first) & (pair_at < 2 * j + near_pos)
            pair_bias = jnp.where(pair_seen, 0.0, hidden_score)
            out = []
            for h in range(heads):
                own = tile(
                    h,
                    own_ref[slot_i, head_rows(1, h), :],
                    own_ref[slot_i, head_rows(2, h), :],
                    tri_ref[...] if diagonal else own_bias,
                    own_grad_ref,
                    slot_i,
                )
                pair = tile(
                    h,
                    pair_ref[slot_i, head_rows(0, h), :],
                    pair_ref[slot_i, head_rows(1, h), :],
                    pair_bias,
                    acc_ref,
                    slot_i,
                )
                out.append(state[h] + own + pair)
            return tuple(out)

        size = own_ref.shape[2]
        state = tuple(jnp.zeros((dim, size), f32) for _ in range(heads))
        state = lax.fori_loop(first // 2, j, lambda i, s: tiles(i, s, False), state)
        state = tiles(j, state, True)
        for h in range(heads):
            query_ref[slot_j, head_rows(0, h), :] = (state[h] * score_scale).astype(bf16)
        return 0

    lax.fori_loop(0, far, query_block, 0)
    pair_grad_ref[...] = acc_ref[...].astype(bf16)


def vmem():
    return pl.BlockSpec(memory_space=pltpu.VMEM)


def attend(where, own, pair, heads, dim):
    far, _, size = own.shape
    rows = heads * dim
    return pl.pallas_call(
        functools.partial(forward_kernel, heads, dim, far),
        name="attend",
        out_shape=(
            jax.ShapeDtypeStruct((far, rows, size), f32),
            jax.ShapeDtypeStruct((far, rows, size), bf16),
            jax.ShapeDtypeStruct((far, 8, size), f32),
        ),
        in_specs=[pl.BlockSpec(memory_space=pltpu.SMEM), vmem(), vmem()],
        out_specs=(vmem(), vmem(), vmem()),
        scratch_shapes=[pltpu.VMEM((size, size), f32)],
        cost_estimate=pl.CostEstimate(
            flops=16 * heads * 4 * dim * size * size,
            bytes_accessed=2 * own.size + 2 * pair.size + 6 * far * rows * size,
            transcendentals=16 * heads * size * size,
        ),
    )(where, own, pair)


def attend_back(where, own, pair, grad, out, lse, heads, dim):
    far, _, size = own.shape
    rows = heads * dim
    return pl.pallas_call(
        functools.partial(backward_kernel, heads, dim, far),
        name="attend_back",
        out_shape=(
            jax.ShapeDtypeStruct((far, rows, size), bf16),
            jax.ShapeDtypeStruct((far, 2 * rows, size), f32),
            jax.ShapeDtypeStruct((far, 2 * rows, size), bf16),
        ),
        in_specs=[pl.BlockSpec(memory_space=pltpu.SMEM)] + [vmem()] * 5,
        out_specs=(vmem(), vmem(), vmem()),
        scratch_shapes=[
            pltpu.VMEM((size, size), f32),
            pltpu.VMEM((far, 2 * rows, size), f32),
        ],
        cost_estimate=pl.CostEstimate(
            flops=16 * heads * 10 * dim * size * size,
            bytes_accessed=2 * own.size + 2 * pair.size + 18 * far * rows * size,
            transcendentals=16 * heads * size * size,
        ),
    )(where, own, pair, grad, out, lse)


def per_device(
    sizes,
    inputs,
    doc_ids,
    cotangent,
    ln1_gain,
    ln1_shift,
    w_qkv,
    b_query,
    b_value,
    w_attn_out,
    b_attn_out,
    ln2_gain,
    ln2_shift,
    w_fc,
    b_fc,
    w_mlp_out,
    b_mlp_out,
):
    order_one, order_two = step_orders(sizes)
    tokens = inputs[0]
    grad_out = cotangent[0]
    group_docs = doc_ids[0]
    tok_count, width = tokens.shape
    dim = width // HEADS
    seq = sizes["seq"]
    far = seq // 2
    heads = HEADS // far
    rows = heads * dim
    position = lax.axis_index("seq")
    far_pos, near_pos = position // 2, position % 2

    shard_rows = w_qkv.shape[0]
    small = jnp.stack(
        [ln1_gain, ln1_shift, b_query, b_value, b_attn_out, ln2_gain, ln2_shift, b_mlp_out], axis=1
    )
    small = jnp.concatenate([small, b_fc.reshape(shard_rows, -1)], axis=1)
    small_count = small.shape[1]
    small = jnp.pad(small, ((0, 0), (0, LANES - small_count)))
    half = w_qkv.shape[1] // 2

    with jax.named_scope("gather_qkv"):
        qkv_one = gather(w_qkv[:, :half], order_one, sizes)
        qkv_two = gather(jnp.concatenate([w_qkv[:, half:], small], axis=1), order_two, sizes)
    with jax.named_scope("gather_rest"):
        proj_full = gather(w_attn_out, order_one, sizes)
        fc_full = gather(w_fc, order_one, sizes)
        out_full = gather(w_mlp_out, order_two, sizes)

    small_cols = qkv_two[:, half:].astype(f32)
    qkv_two = qkv_two[:, :half]
    small_rows = small_cols.T
    gain_one, shift_one = small_rows[0:1], small_rows[1:2]
    proj_bias, gain_two, shift_two, out_bias = (small_rows[n : n + 1] for n in (4, 5, 6, 7))
    fc_bias = small_cols[:, 8:small_count].reshape(1, -1)

    block_docs = group_docs[::tok_count]
    own_blocks = 2 * jnp.arange(far, dtype=jnp.int32) + near_pos
    own_docs = jnp.take(block_docs, own_blocks)
    first_blocks = jnp.sum(
        (block_docs[None, :] < own_docs[:, None]).astype(jnp.int32), axis=1, dtype=jnp.int32
    )
    where = jnp.concatenate([jnp.stack([far_pos, near_pos]), first_blocks]).astype(jnp.int32)

    def shift_far(value, shift):
        return lax.ppermute(
            value, "seq", [(i, (i + 2 * shift) % seq) for i in range(seq)]
        )

    def pick(blocks, index):
        return lax.dynamic_index_in_dim(blocks, lax.rem(index, far), 0, keepdims=False)

    def spread(blocks):
        return [pick(blocks, far_pos)] + [
            shift_far(pick(blocks, far_pos + s), s) for s in range(1, far)
        ]

    def collect(slots):
        got = [slots[0]] + [shift_far(slots[s], far - s) for s in range(1, far)]
        return jnp.stack([pick(jnp.stack(got), g - far_pos + far) for g in range(far)])

    def to_pair(value):
        return lax.ppermute(value, "seq", [(i, i ^ 1) for i in range(seq)])

    normed_in, normal_one, inverse_one = layer_norm(tokens, gain_one, shift_one)
    attn_in = normed_in.astype(bf16)
    bias_cols = jnp.concatenate(
        [small_cols[:, 2:3], jnp.zeros((width, 1), f32), small_cols[:, 3:4]], axis=0
    )
    with jax.named_scope("qkv"):
        qkv_t = jnp.concatenate([dot(qkv_one, attn_in, 0, 1), dot(qkv_two, attn_in, 0, 1)], axis=0)
        qkv_t = (qkv_t + bias_cols).astype(bf16)
    parts = qkv_t.reshape(3, far, rows, tok_count)
    with jax.named_scope("spread_qkv"):
        key_slots = spread(jnp.concatenate([parts[1], parts[2]], axis=1))
        query_slots = spread(parts[0])
        pair_slots = [to_pair(v) for v in key_slots]
    own = jnp.concatenate([jnp.stack(query_slots), jnp.stack(key_slots)], axis=1)
    pair = jnp.stack(pair_slots)
    head_out, head_out_bf, lse = attend(where, own, pair, heads, dim)
    with jax.named_scope("collect_out"):
        attended_t = collect([head_out_bf[s] for s in range(far)]).reshape(width, tok_count)

    resid_one = tokens + dot(attended_t, proj_full, 0, 0) + proj_bias
    normed_mid, normal_two, inverse_two = layer_norm(resid_one, gain_two, shift_two)
    mlp_in = normed_mid.astype(bf16)
    hidden_pre = dot(mlp_in, fc_full, 1, 0) + fc_bias
    hidden_act, hidden_slope = gelu_pair(hidden_pre)
    hidden_bf = hidden_act.astype(bf16)
    result = resid_one + dot(hidden_bf, out_full, 1, 0) + out_bias

    grad_bf = grad_out.astype(bf16)
    g_out_b = jnp.sum(grad_out, axis=0)
    grad_hidden = dot(grad_bf, out_full, 1, 1) * hidden_slope
    hidden_grad_bf = grad_hidden.astype(bf16)
    g_fc_b = jnp.sum(grad_hidden, axis=0)
    grad_mid = dot(hidden_grad_bf, fc_full, 1, 1)
    g_gain_two = jnp.sum(grad_mid * normal_two, axis=0)
    g_shift_two = jnp.sum(grad_mid, axis=0)
    grad_resid = grad_out + norm_back(grad_mid, normal_two, inverse_two, gain_two)
    resid_bf = grad_resid.astype(bf16)
    g_proj_b = jnp.sum(grad_resid, axis=0)
    grad_att_t = dot(proj_full, resid_bf, 1, 1).astype(bf16)
    with jax.named_scope("spread_grad"):
        grad_slots = jnp.stack(spread(grad_att_t.reshape(far, rows, tok_count)))

    with jax.named_scope("scatter_rest"):
        g_out_w = dot(hidden_bf, grad_bf, 0, 0).astype(bf16)
        g_out_w = scatter_sum(g_out_w, order_one, sizes, bf16)
        g_fc_w = dot(mlp_in, hidden_grad_bf, 0, 0).astype(bf16)
        g_fc_w = scatter_sum(g_fc_w, order_two, sizes, bf16)
        g_proj_w = dot(attended_t, resid_bf, 1, 0).astype(bf16)
        g_proj_w = scatter_sum(g_proj_w, order_one, sizes, bf16)

    query_back, own_back, pair_back = attend_back(
        where, own, pair, grad_slots, head_out, lse, heads, dim
    )
    with jax.named_scope("collect_grad"):
        from_pair = [to_pair(pair_back[s]) for s in range(far)]
        query_grad = collect([query_back[s] for s in range(far)])
        key_grad = collect(
            [(own_back[s] + from_pair[s].astype(f32)).astype(bf16) for s in range(far)]
        )
    qkv_grad_t = jnp.concatenate(
        [
            query_grad.reshape(width, tok_count),
            key_grad[:, :rows].reshape(width, tok_count),
            key_grad[:, rows:].reshape(width, tok_count),
        ],
        axis=0,
    )
    with jax.named_scope("scatter_qkv"):
        g_qkv_one = dot(attn_in, qkv_grad_t[:half], 0, 1).astype(bf16)
        g_qkv_one = scatter_sum(g_qkv_one, order_one, sizes, bf16)
        g_qkv_two = dot(attn_in, qkv_grad_t[half:], 0, 1).astype(bf16)
        g_qkv_two = scatter_sum(g_qkv_two, order_two, sizes, bf16)
    grad_first = dot(qkv_grad_t[:half], qkv_one, 0, 1) + dot(qkv_grad_t[half:], qkv_two, 0, 1)
    g_query_b = jnp.sum(qkv_grad_t[:width].astype(f32), axis=1, keepdims=True)
    g_value_b = jnp.sum(qkv_grad_t[2 * width :].astype(f32), axis=1, keepdims=True)
    g_gain_one = jnp.sum(grad_first * normal_one, axis=0)
    g_shift_one = jnp.sum(grad_first, axis=0)
    grad_input = grad_resid + norm_back(grad_first, normal_one, inverse_one, gain_one)

    with jax.named_scope("scatter_small"):
        row_sums = jnp.stack(
            [g_gain_one, g_shift_one, g_proj_b, g_gain_two, g_shift_two, g_out_b]
        ).T
        sums = jnp.concatenate(
            [row_sums, g_query_b, g_value_b, g_fc_b.reshape(width, -1)], axis=1
        )
        sums = jnp.pad(sums, ((0, 0), (0, LANES - sums.shape[1])))
        sums = scatter_sum(sums, order_one, sizes, f32)
    return (
        result[None],
        grad_input[None],
        sums[:, 0],
        sums[:, 1],
        jnp.concatenate([g_qkv_one, g_qkv_two], axis=1),
        sums[:, 6],
        sums[:, 7],
        g_proj_w,
        sums[:, 2],
        sums[:, 3],
        sums[:, 4],
        g_fc_w,
        sums[:, 8:small_count].reshape(-1),
        g_out_w,
        sums[:, 5],
    )


def solution(mesh):
    vector, matrix = P(("seq", "dp")), P(("seq", "dp"), None)
    block = P("dp", "seq", None)
    in_specs = (
        block,
        P("dp", None),
        block,
        vector,
        vector,
        matrix,
        vector,
        vector,
        matrix,
        vector,
        vector,
        vector,
        matrix,
        vector,
        matrix,
        vector,
    )
    out_specs = (
        block,
        block,
        vector,
        vector,
        matrix,
        vector,
        vector,
        matrix,
        vector,
        vector,
        vector,
        matrix,
        vector,
        matrix,
        vector,
    )
    body = functools.partial(per_device, dict(mesh.shape))
    return jax.shard_map(body, mesh=mesh, in_specs=in_specs, out_specs=out_specs, check_vma=False)
```

```python
import functools

import jax
import jax.numpy as jnp
from jax import lax
from jax.experimental import pallas as pl
from jax.experimental.pallas import tpu as pltpu
from jax.sharding import PartitionSpec as P


HEADS = 12
LANES = 128

norm_eps = 1e-05
gelu_root = 0.7978845608028654
gelu_cube = 0.044715
score_scale = 0.125
hidden_score = -1e30


bf16 = jnp.bfloat16
f32 = jnp.float32


def layer_norm(values, gain, shift):
    average = jnp.mean(values, axis=-1, keepdims=True)
    centred = values - average
    variance = jnp.mean(centred * centred, axis=-1, keepdims=True)
    inverse = lax.rsqrt(variance + norm_eps)
    normed = centred * inverse
    return (normed * gain + shift, normed, inverse)


def norm_back(grad_out, normed, inverse, gain):
    scaled = grad_out * gain
    first = jnp.mean(scaled, axis=-1, keepdims=True)
    second = jnp.mean(scaled * normed, axis=-1, keepdims=True)
    return inverse * (scaled - first - normed * second)


def gelu_pair(values):
    inner = gelu_root * (values + gelu_cube * values * values * values)
    tangent = jnp.tanh(inner)
    output = 0.5 * values * (1.0 + tangent)
    slope = 0.5 * (1.0 + tangent) + 0.5 * values * (1.0 - tangent * tangent) * gelu_root * (
        1.0 + 3.0 * gelu_cube * values * values
    )
    return (output, slope)


def dot(left, right, left_dim, right_dim):
    return lax.dot_general(
        left, right, (((left_dim,), (right_dim,)), ((), ())), preferred_element_type=f32
    )


def bits_of(sizes):
    out = []
    for axis in ("seq", "dp"):
        bit = sizes[axis] // 2
        while bit >= 1:
            out.append((axis, bit))
            bit //= 2
    return out


def step_orders(sizes):
    order = bits_of(sizes)
    seq_bits = [s for s in order if s[0] == "seq"]
    dp_bits = [s for s in order if s[0] == "dp"]
    far, near = seq_bits[:-1], seq_bits[-1:]
    side, core = dp_bits[:-1], dp_bits[-1:]
    return (far + near + side + core, far + side + near + core)


def own_bit(step):
    axis, bit = step
    return (lax.axis_index(axis) // bit) % 2


def exchange(value, step, sizes):
    axis, bit = step
    return lax.ppermute(value, axis, [(i, i ^ bit) for i in range(sizes[axis])])


def gather(shard, steps, sizes):
    place = {step: n for n, step in enumerate(bits_of(sizes))}
    have, value = [], shard
    for step in steps:
        other = exchange(value, step, sizes)
        at = sum(1 for m in have if m < place[step])
        have.append(place[step])
        mine, other = jnp.expand_dims(value, at), jnp.expand_dims(other, at)
        shape = mine.shape[:at] + (2,) + mine.shape[at + 1 :]
        side = lax.broadcasted_iota(jnp.int32, shape, at)
        value = jnp.where(side == own_bit(step), mine, other)
    return lax.optimization_barrier(value.reshape(-1, shard.shape[1]))


def scatter_sum(full, steps, sizes):
    order = bits_of(sizes)
    count = 2 ** len(order)
    value = full.reshape((2,) * len(order) + (full.shape[0] // count,) + full.shape[1:])
    left = list(order)
    for step in reversed(steps):
        at = left.index(step)
        left.remove(step)
        low = lax.index_in_dim(value, 0, at, keepdims=False)
        high = lax.index_in_dim(value, 1, at, keepdims=False)
        upper = own_bit(step) == 1
        got = exchange(jnp.where(upper, low, high), step, sizes)
        value = jnp.where(upper, high, low).astype(f32) + got.astype(f32)
        if left:
            value = value.astype(bf16)
    return value


def scatter_sorted(send, keep, steps, sizes):
    for n, step in enumerate(reversed(steps)):
        got = exchange(send, step, sizes)
        total = keep.astype(f32) + got.astype(f32)
        if n < len(steps) - 1:
            rows = total.shape[0] // 2
            send, keep = total[:rows].astype(bf16), total[rows:].astype(bf16)
    return total


def send_order(steps, sizes, width):
    order = bits_of(sizes)
    count = len(order)
    rows = width // 2**count
    column = lax.broadcasted_iota(jnp.int32, (1, width), 1)
    at, inside = column // rows, column % rows
    owner = lax.axis_index("seq") * sizes["dp"] + lax.axis_index("dp")
    for n, step in enumerate(reversed(steps)):
        other = 1 - (at >> (count - 1 - n)) % 2
        owner = owner ^ (other << (count - 1 - order.index(step)))
    row = lax.broadcasted_iota(jnp.int32, (width, width), 0)
    return (row == owner * rows + inside).astype(bf16)


def block_slot(far_pos, index, far):
    return lax.rem(far_pos - index + far, far)


def triangle(size):
    key_pos = lax.broadcasted_iota(jnp.int32, (size, size), 0)
    query_pos = lax.broadcasted_iota(jnp.int32, (size, size), 1)
    return jnp.where(key_pos <= query_pos, 0.0, hidden_score)


def forward_kernel(heads, dim, far, where_ref, own_ref, pair_ref, out_ref, out_bf_ref, lse_ref, tri_ref):
    far_pos, near_pos = where_ref[0], where_ref[1]
    rows = heads * dim
    tri_ref[...] = triangle(tri_ref.shape[0])

    def head_rows(part, head):
        return pl.ds(part * rows + head * dim, dim)

    def query_block(j, _):
        first = where_ref[2 + j]
        slot_j = block_slot(far_pos, j, far)
        queries = [
            own_ref[slot_j, head_rows(0, h), :] * jnp.asarray(score_scale, bf16)
            for h in range(heads)
        ]

        def tiles(i, state):
            slot_i = block_slot(far_pos, i, far)
            own_at, pair_at = 2 * i + near_pos, 2 * i + 1 - near_pos
            own_bias = jnp.where(own_at >= first, 0.0, hidden_score)
            own_bias = jnp.where(i == j, tri_ref[...], own_bias)
            pair_seen = (pair_at >= first) & (pair_at < 2 * j + near_pos)
            pair_bias = jnp.where(pair_seen, 0.0, hidden_score)
            out = []
            for h in range(heads):
                top, total, acc = state[h]
                own = dot(own_ref[slot_i, head_rows(1, h), :], queries[h], 0, 0)
                own = own + own_bias
                pair = dot(pair_ref[slot_i, head_rows(0, h), :], queries[h], 0, 0) + pair_bias
                new_top = jnp.maximum(top, jnp.max(jnp.maximum(own, pair), axis=0, keepdims=True))
                own = jnp.exp(own - new_top)
                pair = jnp.exp(pair - new_top)
                shrink = jnp.exp(top - new_top)
                total = total * shrink + jnp.sum(own + pair, axis=0, keepdims=True)
                acc = (
                    acc * shrink
                    + dot(own_ref[slot_i, head_rows(2, h), :], own.astype(bf16), 1, 0)
                    + dot(pair_ref[slot_i, head_rows(1, h), :], pair.astype(bf16), 1, 0)
                )
                out.append((new_top, total, acc))
            return tuple(out)

        size = own_ref.shape[2]
        state = tuple(
            (
                jnp.full((1, size), hidden_score, f32),
                jnp.zeros((1, size), f32),
                jnp.zeros((dim, size), f32),
            )
            for _ in range(heads)
        )
        state = lax.fori_loop(first // 2, j + 1, tiles, state)
        for h in range(heads):
            top, total, acc = state[h]
            done = acc / total
            out_ref[slot_j, pl.ds(h * dim, dim), :] = done
            out_bf_ref[slot_j, pl.ds(h * dim, dim), :] = done.astype(bf16)
            lse_ref[slot_j, pl.ds(h, 1), :] = top + jnp.log(total)
        return 0

    lax.fori_loop(0, far, query_block, 0)


def backward_kernel(
    heads, dim, far,
    where_ref, own_ref, pair_ref, grad_ref, out_ref, lse_ref,
    query_ref, own_grad_ref, pair_grad_ref, tri_ref, acc_ref,
):
    far_pos, near_pos = where_ref[0], where_ref[1]
    rows = heads * dim
    tri_ref[...] = triangle(tri_ref.shape[0])
    own_grad_ref[...] = jnp.zeros(own_grad_ref.shape, f32)
    acc_ref[...] = jnp.zeros(acc_ref.shape, f32)

    def head_rows(part, head):
        return pl.ds(part * rows + head * dim, dim)

    def query_block(j, _):
        first = where_ref[2 + j]
        slot_j = block_slot(far_pos, j, far)
        queries = [
            own_ref[slot_j, head_rows(0, h), :] * jnp.asarray(score_scale, bf16)
            for h in range(heads)
        ]
        grads = [grad_ref[slot_j, head_rows(0, h), :] for h in range(heads)]
        deltas = [
            jnp.sum(grads[h].astype(f32) * out_ref[slot_j, head_rows(0, h), :], axis=0, keepdims=True)
            for h in range(heads)
        ]
        lses = [lse_ref[slot_j, pl.ds(h, 1), :] for h in range(heads)]

        def tile(h, keys, vals, bias, into, slot_i):
            scores = dot(keys, queries[h], 0, 0)
            prob = jnp.exp(scores + bias - lses[h])
            grad_prob = dot(vals, grads[h], 0, 0)
            grad_score = (prob * (grad_prob - deltas[h])).astype(bf16)
            into[slot_i, head_rows(0, h), :] += dot(queries[h], grad_score, 1, 1)
            into[slot_i, head_rows(1, h), :] += dot(grads[h], prob.astype(bf16), 1, 1)
            return dot(keys, grad_score, 1, 0)

        def tiles(i, state, diagonal):
            slot_i = block_slot(far_pos, i, far)
            own_at, pair_at = 2 * i + near_pos, 2 * i + 1 - near_pos
            own_bias = jnp.where(own_at >= first, 0.0, hidden_score)
            own_bias = tri_ref[...] if diagonal else own_bias
            pair_seen = (pair_at >= first) & (pair_at < 2 * j + near_pos)
            pair_bias = jnp.where(pair_seen, 0.0, hidden_score)
            out = []
            for h in range(heads):
                own = tile(
                    h,
                    own_ref[slot_i, head_rows(1, h), :],
                    own_ref[slot_i, head_rows(2, h), :],
                    own_bias,
                    own_grad_ref,
                    slot_i,
                )
                pair = tile(
                    h,
                    pair_ref[slot_i, head_rows(0, h), :],
                    pair_ref[slot_i, head_rows(1, h), :],
                    pair_bias,
                    acc_ref,
                    slot_i,
                )
                out.append(state[h] + own + pair)
            return tuple(out)

        size = own_ref.shape[2]
        state = tuple(jnp.zeros((dim, size), f32) for _ in range(heads))
        state = lax.fori_loop(first // 2, j, lambda i, s: tiles(i, s, False), state)
        state = tiles(j, state, True)
        for h in range(heads):
            query_ref[slot_j, head_rows(0, h), :] = (state[h] * score_scale).astype(bf16)
        return 0

    lax.fori_loop(0, far, query_block, 0)
    pair_grad_ref[...] = acc_ref[...].astype(bf16)


def vmem():
    return pl.BlockSpec(memory_space=pltpu.VMEM)


def attend(where, own, pair, heads, dim):
    far, _, size = own.shape
    rows = heads * dim
    return pl.pallas_call(
        functools.partial(forward_kernel, heads, dim, far),
        name="attend",
        out_shape=(
            jax.ShapeDtypeStruct((far, rows, size), f32),
            jax.ShapeDtypeStruct((far, rows, size), bf16),
            jax.ShapeDtypeStruct((far, 8, size), f32),
        ),
        in_specs=[pl.BlockSpec(memory_space=pltpu.SMEM), vmem(), vmem()],
        out_specs=(vmem(), vmem(), vmem()),
        scratch_shapes=[pltpu.VMEM((size, size), f32)],
        cost_estimate=pl.CostEstimate(
            flops=16 * heads * 4 * dim * size * size,
            bytes_accessed=2 * own.size + 2 * pair.size + 6 * far * rows * size,
            transcendentals=16 * heads * size * size,
        ),
    )(where, own, pair)


def attend_back(where, own, pair, grad, out, lse, heads, dim):
    far, _, size = own.shape
    rows = heads * dim
    return pl.pallas_call(
        functools.partial(backward_kernel, heads, dim, far),
        name="attend_back",
        out_shape=(
            jax.ShapeDtypeStruct((far, rows, size), bf16),
            jax.ShapeDtypeStruct((far, 2 * rows, size), f32),
            jax.ShapeDtypeStruct((far, 2 * rows, size), bf16),
        ),
        in_specs=[pl.BlockSpec(memory_space=pltpu.SMEM)] + [vmem()] * 5,
        out_specs=(vmem(), vmem(), vmem()),
        scratch_shapes=[
            pltpu.VMEM((size, size), f32),
            pltpu.VMEM((far, 2 * rows, size), f32),
        ],
        cost_estimate=pl.CostEstimate(
            flops=16 * heads * 10 * dim * size * size,
            bytes_accessed=2 * own.size + 2 * pair.size + 18 * far * rows * size,
            transcendentals=16 * heads * size * size,
        ),
    )(where, own, pair, grad, out, lse)


def per_device(
    sizes,
    inputs,
    doc_ids,
    cotangent,
    ln1_gain,
    ln1_shift,
    w_qkv,
    b_query,
    b_value,
    w_attn_out,
    b_attn_out,
    ln2_gain,
    ln2_shift,
    w_fc,
    b_fc,
    w_mlp_out,
    b_mlp_out,
):
    order_one, order_two = step_orders(sizes)
    tokens = inputs[0]
    grad_out = cotangent[0]
    group_docs = doc_ids[0]
    tok_count, width = tokens.shape
    dim = width // HEADS
    seq = sizes["seq"]
    far = seq // 2
    heads = HEADS // far
    rows = heads * dim
    position = lax.axis_index("seq")
    far_pos, near_pos = position // 2, position % 2

    shard_rows = w_qkv.shape[0]
    small = jnp.stack(
        [ln1_gain, ln1_shift, b_query, b_value, b_attn_out, ln2_gain, ln2_shift, b_mlp_out], axis=1
    )
    small = jnp.concatenate([small, b_fc.reshape(shard_rows, -1)], axis=1)
    small_count = small.shape[1]
    small = jnp.pad(small, ((0, 0), (0, LANES - small_count)))
    half = w_qkv.shape[1] // 2

    qkv_one = gather(w_qkv[:, :half], order_one, sizes)
    qkv_two = gather(jnp.concatenate([w_qkv[:, half:], small], axis=1), order_two, sizes)
    fc_full = gather(w_fc, order_one, sizes)
    out_full = gather(w_mlp_out, order_two, sizes)
    proj_full = gather(w_attn_out, order_two, sizes)

    small_cols = qkv_two[:, half:].astype(f32)
    small_rows = small_cols.T
    gain_one, shift_one = small_rows[0:1], small_rows[1:2]
    proj_bias, gain_two, shift_two, out_bias = (small_rows[n : n + 1] for n in (4, 5, 6, 7))
    fc_bias = small_cols[:, 8:small_count].reshape(1, -1)

    block_docs = group_docs[::tok_count]
    own_blocks = 2 * jnp.arange(far, dtype=jnp.int32) + near_pos
    own_docs = jnp.take(block_docs, own_blocks)
    first_blocks = jnp.sum(
        (block_docs[None, :] < own_docs[:, None]).astype(jnp.int32), axis=1, dtype=jnp.int32
    )
    where = jnp.concatenate([jnp.stack([far_pos, near_pos]), first_blocks]).astype(jnp.int32)

    def shift_far(value, shift):
        return lax.ppermute(
            value, "seq", [(i, (i + 2 * shift) % seq) for i in range(seq)]
        )

    def pick(blocks, index):
        return lax.dynamic_index_in_dim(blocks, lax.rem(index, far), 0, keepdims=False)

    def spread(blocks):
        out = [pick(blocks, far_pos)]
        for s in range(1, far):
            out.append(shift_far(pick(blocks, far_pos + s), s))
        return out

    def collect(slots):
        got = [slots[0]]
        for s in range(1, far):
            got.append(shift_far(slots[s], far - s))
        return jnp.stack([pick(jnp.stack(got), g - far_pos + far) for g in range(far)])

    def to_pair(value):
        return lax.ppermute(value, "seq", [(i, i ^ 1) for i in range(seq)])

    normed_in, normal_one, inverse_one = layer_norm(tokens, gain_one, shift_one)
    attn_in = normed_in.astype(bf16)
    bias_cols = jnp.concatenate(
        [small_cols[:, 2:3], jnp.zeros((width, 1), f32), small_cols[:, 3:4]], axis=0
    )
    qkv_t = jnp.concatenate(
        [dot(qkv_one, attn_in, 0, 1), dot(qkv_two, attn_in, 0, 1)[:half]], axis=0
    )
    qkv_t = (qkv_t + bias_cols).astype(bf16)
    parts = qkv_t.reshape(3, far, rows, tok_count)
    key_slots = spread(jnp.concatenate([parts[1], parts[2]], axis=1))
    query_slots = spread(parts[0])
    pair_slots = []
    for value in key_slots:
        pair_slots.append(to_pair(value))
    own = jnp.concatenate([jnp.stack(query_slots), jnp.stack(key_slots)], axis=1)
    pair = jnp.stack(pair_slots)
    head_out, head_out_bf, lse = attend(where, own, pair, heads, dim)
    attended_t = collect([head_out_bf[s] for s in range(far)]).reshape(width, tok_count)

    resid_one = tokens + dot(attended_t, proj_full, 0, 0) + proj_bias
    normed_mid, normal_two, inverse_two = layer_norm(resid_one, gain_two, shift_two)
    mlp_in = normed_mid.astype(bf16)
    hidden_pre = dot(mlp_in, fc_full, 1, 0) + fc_bias
    hidden_act, hidden_slope = gelu_pair(hidden_pre)
    hidden_bf = hidden_act.astype(bf16)
    result = resid_one + dot(hidden_bf, out_full, 1, 0) + out_bias

    grad_bf = grad_out.astype(bf16)
    g_out_b = jnp.sum(grad_out, axis=0)
    grad_hidden = dot(grad_bf, out_full, 1, 1) * hidden_slope
    hidden_grad_bf = grad_hidden.astype(bf16)
    g_fc_b = jnp.sum(grad_hidden, axis=0)
    grad_mid = dot(hidden_grad_bf, fc_full, 1, 1)
    g_gain_two = jnp.sum(grad_mid * normal_two, axis=0)
    g_shift_two = jnp.sum(grad_mid, axis=0)
    grad_resid = grad_out + norm_back(grad_mid, normal_two, inverse_two, gain_two)
    resid_bf = grad_resid.astype(bf16)
    g_proj_b = jnp.sum(grad_resid, axis=0)
    grad_att_t = dot(proj_full, resid_bf, 1, 1).astype(bf16)
    grad_slots = jnp.stack(spread(grad_att_t.reshape(far, rows, tok_count)))

    sort_one, sort_two = (send_order(o, sizes, width) for o in (order_one, order_two))
    part = width // 2

    g_out_w = dot(hidden_bf, grad_bf, 0, 0).astype(bf16)
    g_out_w = scatter_sum(g_out_w, order_one, sizes)
    mlp_sorted = dot(mlp_in, sort_one, 1, 0).astype(bf16)
    att_sorted = dot(sort_one, attended_t, 0, 0).astype(bf16)
    fc_cols = hidden_grad_bf.shape[1]

    def fc_proj(low, high):
        g_fc = dot(mlp_sorted[:, low:high], hidden_grad_bf, 0, 0).astype(bf16)
        g_proj = dot(att_sorted[low:high], resid_bf, 1, 0).astype(bf16)
        return jnp.concatenate([g_fc, g_proj], axis=1)

    g_fc_proj = scatter_sorted(fc_proj(0, part), fc_proj(part, width), order_one, sizes)

    query_back, own_back, pair_back = attend_back(
        where, own, pair, grad_slots, head_out, lse, heads, dim
    )
    from_pair = []
    for n in range(far):
        from_pair.append(to_pair(pair_back[n]))
    query_grad = collect([query_back[s] for s in range(far)])
    key_grad = collect([(own_back[s] + from_pair[s].astype(f32)).astype(bf16) for s in range(far)])
    qkv_grad_t = jnp.concatenate(
        [
            query_grad.reshape(width, tok_count),
            key_grad[:, :rows].reshape(width, tok_count),
            key_grad[:, rows:].reshape(width, tok_count),
        ],
        axis=0,
    )
    sorted_one = dot(attn_in, sort_one, 1, 0).astype(bf16)
    sorted_two = dot(attn_in, sort_two, 1, 0).astype(bf16)
    g_qkv_one = scatter_sorted(
        dot(sorted_one[:, :part], qkv_grad_t[:half], 0, 1).astype(bf16),
        dot(sorted_one[:, part:], qkv_grad_t[:half], 0, 1).astype(bf16),
        order_one,
        sizes,
    )
    grad_first = dot(qkv_grad_t[:half], qkv_one, 0, 1) + dot(
        qkv_grad_t[half:], qkv_two[:, :half], 0, 1
    )
    g_query_b = jnp.sum(qkv_grad_t[:width].astype(f32), axis=1, keepdims=True)
    g_value_b = jnp.sum(qkv_grad_t[2 * width :].astype(f32), axis=1, keepdims=True)
    g_gain_one = jnp.sum(grad_first * normal_one, axis=0)
    g_shift_one = jnp.sum(grad_first, axis=0)
    grad_input = grad_resid + norm_back(grad_first, normal_one, inverse_one, gain_one)

    row_sums = jnp.stack(
        [g_gain_one, g_shift_one, g_proj_b, g_gain_two, g_shift_two, g_out_b]
    ).T
    sums = jnp.concatenate([row_sums, g_query_b, g_value_b, g_fc_b.reshape(width, -1)], axis=1)
    sums = jnp.pad(sums, ((0, 0), (0, LANES - sums.shape[1]))).astype(bf16)
    sums = dot(sort_two, sums, 0, 0).astype(bf16)

    def qkv_sums(low, high):
        g_two = dot(sorted_two[:, low:high], qkv_grad_t[half:], 0, 1).astype(bf16)
        return jnp.concatenate([g_two, sums[low:high]], axis=1)

    g_qkv_two = scatter_sorted(qkv_sums(0, part), qkv_sums(part, width), order_two, sizes)
    g_qkv_two, sums = g_qkv_two[:, :half], g_qkv_two[:, half:]
    return (
        result[None],
        grad_input[None],
        sums[:, 0],
        sums[:, 1],
        jnp.concatenate([g_qkv_one, g_qkv_two], axis=1),
        sums[:, 6],
        sums[:, 7],
        g_fc_proj[:, fc_cols:],
        sums[:, 2],
        sums[:, 3],
        sums[:, 4],
        g_fc_proj[:, :fc_cols],
        sums[:, 8:small_count].reshape(-1),
        g_out_w,
        sums[:, 5],
    )


def solution(mesh):
    vector, matrix = P(("seq", "dp")), P(("seq", "dp"), None)
    block = P("dp", "seq", None)
    in_specs = (
        block,
        P("dp", None),
        block,
        vector,
        vector,
        matrix,
        vector,
        vector,
        matrix,
        vector,
        vector,
        vector,
        matrix,
        vector,
        matrix,
        vector,
    )
    out_specs = (
        block,
        block,
        vector,
        vector,
        matrix,
        vector,
        vector,
        matrix,
        vector,
        vector,
        vector,
        matrix,
        vector,
        matrix,
        vector,
    )

    def body(*args):
        return per_device(dict(mesh.shape), *args)

    return jax.shard_map(body, mesh=mesh, in_specs=in_specs, out_specs=out_specs, check_vma=False)
```

```python
import functools

import jax
import jax.numpy as jnp
from jax import lax
from jax.experimental import pallas as pl
from jax.experimental.pallas import tpu as pltpu
from jax.sharding import PartitionSpec as P


HEADS = 12
LANES = 128

norm_eps = 1e-05
gelu_root = 0.7978845608028654
gelu_cube = 0.044715
score_scale = 0.125
hidden_score = -1e30


bf16 = jnp.bfloat16
f32 = jnp.float32


def layer_norm(values, gain, shift):
    average = jnp.mean(values, axis=-1, keepdims=True)
    centred = values - average
    variance = jnp.mean(centred * centred, axis=-1, keepdims=True)
    inverse = lax.rsqrt(variance + norm_eps)
    normed = centred * inverse
    return (normed * gain + shift, normed, inverse)


def norm_back(grad_out, normed, inverse, gain):
    scaled = grad_out * gain
    first = jnp.mean(scaled, axis=-1, keepdims=True)
    second = jnp.mean(scaled * normed, axis=-1, keepdims=True)
    return inverse * (scaled - first - normed * second)


def gelu_pair(values):
    inner = gelu_root * (values + gelu_cube * values * values * values)
    tangent = jnp.tanh(inner)
    output = 0.5 * values * (1.0 + tangent)
    slope = 0.5 * (1.0 + tangent) + 0.5 * values * (1.0 - tangent * tangent) * gelu_root * (
        1.0 + 3.0 * gelu_cube * values * values
    )
    return (output, slope)


def dot(left, right, left_dim, right_dim):
    return lax.dot_general(
        left, right, (((left_dim,), (right_dim,)), ((), ())), preferred_element_type=f32
    )


def bits_of(sizes):
    out = []
    for axis in ("seq", "dp"):
        bit = sizes[axis] // 2
        while bit >= 1:
            out.append((axis, bit))
            bit //= 2
    return out


def step_orders(sizes):
    order = bits_of(sizes)
    seq_bits = [s for s in order if s[0] == "seq"]
    dp_bits = [s for s in order if s[0] == "dp"]
    far, near = seq_bits[:-1], seq_bits[-1:]
    side, core = dp_bits[:-1], dp_bits[-1:]
    return (far + near + side + core, far + side + near + core)


def own_bit(step):
    axis, bit = step
    return (lax.axis_index(axis) // bit) % 2


def exchange(value, step, sizes):
    axis, bit = step
    return lax.ppermute(value, axis, [(i, i ^ bit) for i in range(sizes[axis])])


def gather(shard, steps, sizes, join=True):
    place = {step: n for n, step in enumerate(bits_of(sizes))}
    have, value = [], shard
    for n, step in enumerate(steps):
        other = exchange(value, step, sizes)
        if n == len(steps) - 1 and not join:
            return (value.reshape((-1,) + shard.shape), other.reshape((-1,) + shard.shape))
        at = sum(1 for m in have if m < place[step])
        have.append(place[step])
        mine, other = jnp.expand_dims(value, at), jnp.expand_dims(other, at)
        shape = mine.shape[:at] + (2,) + mine.shape[at + 1 :]
        side = lax.broadcasted_iota(jnp.int32, shape, at)
        value = jnp.where(side == own_bit(step), mine, other)
    return value.reshape(-1, shard.shape[1])


def scatter_sum(full, steps, sizes):
    order = bits_of(sizes)
    count = 2 ** len(order)
    value = full.reshape((2,) * len(order) + (full.shape[0] // count,) + full.shape[1:])
    left = list(order)
    for step in reversed(steps):
        at = left.index(step)
        left.remove(step)
        low = lax.index_in_dim(value, 0, at, keepdims=False)
        high = lax.index_in_dim(value, 1, at, keepdims=False)
        upper = own_bit(step) == 1
        got = exchange(jnp.where(upper, low, high), step, sizes)
        value = jnp.where(upper, high, low).astype(f32) + got.astype(f32)
        if left:
            value = value.astype(bf16)
    return value


def scatter_sorted(send, keep, steps, sizes):
    for n, step in enumerate(reversed(steps)):
        got = exchange(send, step, sizes)
        total = keep.astype(f32) + got.astype(f32)
        if n < len(steps) - 1:
            rows = total.shape[0] // 2
            send, keep = total[:rows].astype(bf16), total[rows:].astype(bf16)
    return total


def send_order(steps, sizes, width):
    order = bits_of(sizes)
    count = len(order)
    rows = width // 2**count
    column = lax.broadcasted_iota(jnp.int32, (1, width), 1)
    at, inside = column // rows, column % rows
    owner = lax.axis_index("seq") * sizes["dp"] + lax.axis_index("dp")
    for n, step in enumerate(reversed(steps)):
        other = 1 - (at >> (count - 1 - n)) % 2
        owner = owner ^ (other << (count - 1 - order.index(step)))
    row = lax.broadcasted_iota(jnp.int32, (width, width), 0)
    return (row == owner * rows + inside).astype(bf16)


def block_slot(far_pos, index, far):
    return lax.rem(far_pos - index + far, far)


def triangle(size):
    key_pos = lax.broadcasted_iota(jnp.int32, (size, size), 0)
    query_pos = lax.broadcasted_iota(jnp.int32, (size, size), 1)
    return jnp.where(key_pos <= query_pos, 0.0, hidden_score)


def forward_kernel(heads, dim, far, where_ref, *refs):
    query_refs, key_refs, pair_refs = refs[:far], refs[far : 2 * far], refs[2 * far : 3 * far]
    own_ref, pair_ref, out_ref, lse_ref = refs[3 * far : 3 * far + 4]
    slot_refs, tri_ref = refs[3 * far + 4 : 4 * far + 4], refs[4 * far + 4]
    far_pos, near_pos = where_ref[0], where_ref[1]
    rows = heads * dim
    for s in range(far):
        own_ref[s, :rows, :] = query_refs[s][...]
        own_ref[s, rows:, :] = key_refs[s][...]
        pair_ref[s] = pair_refs[s][...]
    tri_ref[0] = jnp.zeros(tri_ref.shape[1:], f32)
    tri_ref[1] = triangle(tri_ref.shape[1])

    def head_rows(part, head):
        return pl.ds(part * rows + head * dim, dim)

    def query_block(j, _):
        first = where_ref[2 + j]
        slot_j = block_slot(far_pos, j, far)
        queries = [
            own_ref[slot_j, head_rows(0, h), :] * jnp.asarray(score_scale, bf16)
            for h in range(heads)
        ]

        def tiles(i, state):
            slot_i = block_slot(far_pos, i, far)
            own_at, pair_at = 2 * i + near_pos, 2 * i + 1 - near_pos
            own_bias = jnp.where(own_at >= first, 0.0, hidden_score)
            diagonal = (i == j).astype(jnp.int32)
            pair_seen = (pair_at >= first) & (pair_at < 2 * j + near_pos)
            pair_bias = jnp.where(pair_seen, 0.0, hidden_score)
            out = []
            for h in range(heads):
                top, total, acc = state[h]
                own = dot(own_ref[slot_i, head_rows(1, h), :], queries[h], 0, 0)
                own = own + tri_ref[diagonal] + own_bias
                pair = dot(pair_ref[slot_i, head_rows(0, h), :], queries[h], 0, 0) + pair_bias
                new_top = jnp.maximum(top, jnp.max(jnp.maximum(own, pair), axis=0, keepdims=True))
                own = jnp.exp(own - new_top)
                pair = jnp.exp(pair - new_top)
                shrink = jnp.exp(top - new_top)
                total = total * shrink + jnp.sum(own + pair, axis=0, keepdims=True)
                acc = (
                    acc * shrink
                    + dot(own_ref[slot_i, head_rows(2, h), :], own.astype(bf16), 1, 0)
                    + dot(pair_ref[slot_i, head_rows(1, h), :], pair.astype(bf16), 1, 0)
                )
                out.append((new_top, total, acc))
            return tuple(out)

        size = own_ref.shape[2]
        state = tuple(
            (
                jnp.full((1, size), hidden_score, f32),
                jnp.zeros((1, size), f32),
                jnp.zeros((dim, size), f32),
            )
            for _ in range(heads)
        )
        state = lax.fori_loop(first // 2, j + 1, tiles, state)
        for h in range(heads):
            top, total, acc = state[h]
            done = acc / total
            out_ref[slot_j, pl.ds(h * dim, dim), :] = done
            lse_ref[slot_j, pl.ds(h, 1), :] = top + jnp.log(total)
        return 0

    lax.fori_loop(0, far, query_block, 0)
    for s in range(far):
        slot_refs[s][...] = out_ref[s].astype(bf16)


def backward_kernel(heads, dim, far, where_ref, own_ref, pair_ref, out_ref, lse_ref, *refs):
    grad_refs, query_refs, pair_grad_refs = refs[:far], refs[far : 2 * far], refs[2 * far : 3 * far]
    own_grad_ref, grad_ref, query_ref, tri_ref, acc_ref = refs[3 * far :]
    far_pos, near_pos = where_ref[0], where_ref[1]
    rows = heads * dim
    for s in range(far):
        grad_ref[s] = grad_refs[s][...]
    tri_ref[0] = jnp.zeros(tri_ref.shape[1:], f32)
    tri_ref[1] = triangle(tri_ref.shape[1])
    own_grad_ref[...] = jnp.zeros(own_grad_ref.shape, f32)
    acc_ref[...] = jnp.zeros(acc_ref.shape, f32)

    def head_rows(part, head):
        return pl.ds(part * rows + head * dim, dim)

    def query_block(j, _):
        first = where_ref[2 + j]
        slot_j = block_slot(far_pos, j, far)
        queries = [
            own_ref[slot_j, head_rows(0, h), :] * jnp.asarray(score_scale, bf16)
            for h in range(heads)
        ]
        grads = [grad_ref[slot_j, head_rows(0, h), :] for h in range(heads)]
        deltas = [
            jnp.sum(grads[h].astype(f32) * out_ref[slot_j, head_rows(0, h), :], axis=0, keepdims=True)
            for h in range(heads)
        ]
        lses = [lse_ref[slot_j, pl.ds(h, 1), :] for h in range(heads)]

        def tile(h, keys, vals, bias, mask, into, slot_i):
            scores = dot(keys, queries[h], 0, 0)
            if mask is not None:
                scores = scores + tri_ref[mask]
            prob = jnp.exp(scores - (lses[h] - bias))
            grad_prob = dot(vals, grads[h], 0, 0)
            grad_score = (prob * (grad_prob - deltas[h])).astype(bf16)
            into[slot_i, head_rows(0, h), :] += dot(queries[h], grad_score, 1, 1)
            into[slot_i, head_rows(1, h), :] += dot(grads[h], prob.astype(bf16), 1, 1)
            return dot(keys, grad_score, 1, 0)

        def tiles(i, state):
            slot_i = block_slot(far_pos, i, far)
            own_at, pair_at = 2 * i + near_pos, 2 * i + 1 - near_pos
            own_bias = jnp.where(own_at >= first, 0.0, hidden_score)
            diagonal = (i == j).astype(jnp.int32)
            pair_seen = (pair_at >= first) & (pair_at < 2 * j + near_pos)
            pair_bias = jnp.where(pair_seen, 0.0, hidden_score)
            out = []
            for h in range(heads):
                own = tile(
                    h,
                    own_ref[slot_i, head_rows(1, h), :],
                    own_ref[slot_i, head_rows(2, h), :],
                    own_bias,
                    diagonal,
                    own_grad_ref,
                    slot_i,
                )
                pair = tile(
                    h,
                    pair_ref[slot_i, head_rows(0, h), :],
                    pair_ref[slot_i, head_rows(1, h), :],
                    pair_bias,
                    None,
                    acc_ref,
                    slot_i,
                )
                out.append(state[h] + own + pair)
            return tuple(out)

        size = own_ref.shape[2]
        state = tuple(jnp.zeros((dim, size), f32) for _ in range(heads))
        state = lax.fori_loop(first // 2, j + 1, tiles, state)
        for h in range(heads):
            query_ref[slot_j, head_rows(0, h), :] = (state[h] * score_scale).astype(bf16)
        return 0

    lax.fori_loop(0, far, query_block, 0)
    for s in range(far):
        query_refs[s][...] = query_ref[s]
        pair_grad_refs[s][...] = acc_ref[s].astype(bf16)


def vmem():
    return pl.BlockSpec(memory_space=pltpu.VMEM)


def attend(where, queries, keys, pairs, heads, dim):
    far, size, rows = len(queries), queries[0].shape[1], heads * dim
    return pl.pallas_call(
        functools.partial(forward_kernel, heads, dim, far),
        name="attend",
        out_shape=(
            jax.ShapeDtypeStruct((far, 3 * rows, size), bf16),
            jax.ShapeDtypeStruct((far, 2 * rows, size), bf16),
            jax.ShapeDtypeStruct((far, rows, size), f32),
            jax.ShapeDtypeStruct((far, 8, size), f32),
        )
        + (jax.ShapeDtypeStruct((rows, size), bf16),) * far,
        in_specs=[pl.BlockSpec(memory_space=pltpu.SMEM)] + [vmem()] * (3 * far),
        out_specs=(vmem(),) * (4 + far),
        scratch_shapes=[pltpu.VMEM((2, size, size), f32)],
        cost_estimate=pl.CostEstimate(
            flops=16 * heads * 4 * dim * size * size,
            bytes_accessed=24 * far * rows * size,
            transcendentals=16 * heads * size * size,
        ),
    )(where, *queries, *keys, *pairs)


def attend_back(where, own, pair, out, lse, grads, heads, dim):
    far, size, rows = len(grads), own.shape[2], heads * dim
    return pl.pallas_call(
        functools.partial(backward_kernel, heads, dim, far),
        name="attend_back",
        out_shape=(jax.ShapeDtypeStruct((rows, size), bf16),) * far
        + (jax.ShapeDtypeStruct((2 * rows, size), bf16),) * far
        + (jax.ShapeDtypeStruct((far, 2 * rows, size), f32),),
        in_specs=[pl.BlockSpec(memory_space=pltpu.SMEM)] + [vmem()] * (4 + far),
        out_specs=(vmem(),) * (2 * far + 1),
        scratch_shapes=[
            pltpu.VMEM((far, rows, size), bf16),
            pltpu.VMEM((far, rows, size), bf16),
            pltpu.VMEM((2, size, size), f32),
            pltpu.VMEM((far, 2 * rows, size), f32),
        ],
        cost_estimate=pl.CostEstimate(
            flops=16 * heads * 10 * dim * size * size,
            bytes_accessed=32 * far * rows * size,
            transcendentals=16 * heads * size * size,
        ),
    )(where, own, pair, out, lse, *grads)


def project_kernel(rows, far, where_ref, tokens_ref, one_ref, two_ref, normed_ref, small_ref, *refs):
    query_refs, key_refs, all_ref = refs[:far], refs[far : 2 * far], refs[2 * far]
    width, half = tokens_ref.shape[1], one_ref.shape[1]
    columns = two_ref[:, half:].astype(f32)
    small = columns.T[: small_ref.shape[0]]
    small_ref[...] = small
    normed = layer_norm(tokens_ref[...], small[0:1], small[1:2])[0].astype(bf16)
    normed_ref[...] = normed
    one = dot(one_ref[...], normed, 0, 1)
    all_ref[:width, :] = (one[:width] + columns[:, 2:3]).astype(bf16)
    all_ref[width:half, :] = one[width:].astype(bf16)
    two = dot(two_ref[:, :half], normed, 0, 1)
    cut = 2 * width - half
    all_ref[half : 2 * width, :] = two[:cut].astype(bf16)
    all_ref[2 * width :, :] = (two[cut:] + columns[:, 3:4]).astype(bf16)
    for s in range(far):
        first = lax.rem(where_ref[0] + s, far) * rows
        for part, ref, at in ((0, query_refs[s], 0), (1, key_refs[s], 0), (2, key_refs[s], rows)):
            start = pl.multiple_of(part * width + first, rows)
            ref[pl.ds(at, rows), :] = all_ref[pl.ds(start, rows), :]


def project(where, tokens, one, two, rows, far):
    size, width = tokens.shape
    return pl.pallas_call(
        functools.partial(project_kernel, rows, far),
        name="project",
        out_shape=(
            jax.ShapeDtypeStruct((size, width), bf16),
            jax.ShapeDtypeStruct((8, width), f32),
        )
        + (jax.ShapeDtypeStruct((rows, size), bf16),) * far
        + (jax.ShapeDtypeStruct((2 * rows, size), bf16),) * far,
        in_specs=[pl.BlockSpec(memory_space=pltpu.SMEM)] + [vmem()] * 3,
        out_specs=(vmem(),) * (2 + 2 * far),
        scratch_shapes=[pltpu.VMEM((3 * width, size), bf16)],
        cost_estimate=pl.CostEstimate(
            flops=6 * size * width * width, bytes_accessed=12 * width * width, transcendentals=0
        ),
    )(where, tokens, one, two)


def middle_kernel(rows, far, pieces, where_ref, tokens_ref, cot_ref, *refs):
    slot_refs = refs[:far]
    proj_ref, small_ref, fc_ref, fc_bias_ref = refs[far : far + 4]
    out_refs = refs[far + 4 : far + 4 + pieces]
    refs = refs[far + 4 + pieces :]
    (result_ref, att_ref, mlp_ref, resid_ref, grad_resid_ref, sums_ref) = refs[:6]
    hidden_ref, hidden_grad_ref, fc_sum_ref = refs[6:9]
    grad_refs = refs[9 : 9 + far]
    normal_ref, inverse_ref, acc_ref, cot_bf_ref, back_ref, out_ref = refs[9 + far :]
    step = pl.program_id(0)

    @pl.when(step == 0)
    def _():
        for s in range(far):
            first = pl.multiple_of(lax.rem(where_ref[0] + s, far) * rows, rows)
            att_ref[pl.ds(first, rows), :] = slot_refs[s][...]
        resid = tokens_ref[...] + dot(att_ref[...], proj_ref[...], 0, 0) + small_ref[4:5]
        normed, normal, inverse = layer_norm(resid, small_ref[5:6], small_ref[6:7])
        mlp_ref[...] = normed.astype(bf16)
        normal_ref[...] = normal
        inverse_ref[...] = jnp.broadcast_to(inverse, inverse_ref.shape)
        result_ref[...] = resid + small_ref[7:8]
        cot_bf_ref[...] = cot_ref[...].astype(bf16)
        acc_ref[...] = jnp.zeros(acc_ref.shape, f32)

    weight_in = fc_ref[...]
    if pieces == 1:
        weight_out = out_refs[0][...]
    else:
        count, piece = out_refs[0].shape[:2]
        for side, ref in enumerate(out_refs):
            core = (where_ref[2 + far] + side) % 2
            for n in range(count):
                start = pl.multiple_of((2 * n + core) * piece, 32)
                out_ref[pl.ds(start, piece), :] = ref[n]
        weight_out = out_ref[...]
    pre = dot(mlp_ref[...], weight_in, 1, 0) + fc_bias_ref[...]
    act, slope = gelu_pair(pre)
    hidden = act.astype(bf16)
    hidden_ref[...] = hidden
    result_ref[...] += dot(hidden, weight_out, 1, 0)
    grad = dot(cot_bf_ref[...], weight_out, 1, 1) * slope
    fc_sum_ref[...] = jnp.sum(grad, axis=0, keepdims=True)
    grad = grad.astype(bf16)
    hidden_grad_ref[...] = grad
    acc_ref[...] += dot(grad, weight_in, 1, 1)

    @pl.when(step == pl.num_programs(0) - 1)
    def _():
        normal, grad_mid, cot = normal_ref[...], acc_ref[...], cot_ref[...]
        back = norm_back(grad_mid, normal, inverse_ref[:, 0:1], small_ref[5:6])
        grad_resid = cot + back
        grad_resid_ref[...] = grad_resid
        resid_bf = grad_resid.astype(bf16)
        resid_ref[...] = resid_bf
        back_ref[...] = dot(proj_ref[...], resid_bf, 1, 1).astype(bf16)
        for s in range(far):
            first = pl.multiple_of(lax.rem(where_ref[0] + s, far) * rows, rows)
            grad_refs[s][...] = back_ref[pl.ds(first, rows), :]
        totals = (grad_resid, grad_mid * normal, grad_mid, cot)
        sums_ref[0:4, :] = jnp.concatenate(
            [jnp.sum(value, axis=0, keepdims=True) for value in totals], axis=0
        )
        sums_ref[4:8, :] = jnp.zeros((4, sums_ref.shape[1]), f32)


def middle(where, tokens, cot, slots, fc_proj, small, out, fc_bias, rows):
    far, (size, width), hidden = len(slots), tokens.shape, fc_bias.shape[1]
    cut = width
    steps = hidden // cut

    def whole(shape):
        return pl.BlockSpec(shape, lambda f: (0,) * len(shape))

    token_spec, rows_spec = whole((size, width)), whole((rows, size))
    hidden_spec = pl.BlockSpec((size, cut), lambda f: (0, f))
    bias_spec = pl.BlockSpec((1, cut), lambda f: (0, f))
    if len(out) == 1:
        out_specs = [pl.BlockSpec((cut, width), lambda f: (f, 0))]
    else:
        piece = out[0].shape[1]
        out_specs = [pl.BlockSpec((cut // piece // 2, piece, width), lambda f: (f, 0, 0))] * 2
    return pl.pallas_call(
        functools.partial(middle_kernel, rows, far, len(out)),
        name="middle",
        grid=(steps,),
        out_shape=(
            jax.ShapeDtypeStruct((size, width), f32),
            jax.ShapeDtypeStruct((width, size), bf16),
            jax.ShapeDtypeStruct((size, width), bf16),
            jax.ShapeDtypeStruct((size, width), bf16),
            jax.ShapeDtypeStruct((size, width), f32),
            jax.ShapeDtypeStruct((8, width), f32),
            jax.ShapeDtypeStruct((size, hidden), bf16),
            jax.ShapeDtypeStruct((size, hidden), bf16),
            jax.ShapeDtypeStruct((1, hidden), f32),
        )
        + (jax.ShapeDtypeStruct((rows, size), bf16),) * far,
        in_specs=[pl.BlockSpec(memory_space=pltpu.SMEM), token_spec, token_spec]
        + [rows_spec] * far
        + [
            pl.BlockSpec((width, width), lambda f: (0, hidden // width)),
            whole((8, width)),
            pl.BlockSpec((width, cut), lambda f: (0, f)),
            bias_spec,
        ]
        + out_specs,
        out_specs=(
            token_spec,
            whole((width, size)),
            token_spec,
            token_spec,
            token_spec,
            whole((8, width)),
            hidden_spec,
            hidden_spec,
            bias_spec,
        )
        + (rows_spec,) * far,
        scratch_shapes=[
            pltpu.VMEM((size, width), f32),
            pltpu.VMEM((size, LANES), f32),
            pltpu.VMEM((size, width), f32),
            pltpu.VMEM((size, width), bf16),
            pltpu.VMEM((width, size), bf16),
            pltpu.VMEM((cut, width), bf16),
        ],
        cost_estimate=pl.CostEstimate(
            flops=8 * size * width * hidden + 4 * size * width * width,
            bytes_accessed=4 * width * hidden + 4 * size * hidden + 24 * size * width,
            transcendentals=size * hidden,
        ),
    )(where, tokens, cot, *slots, fc_proj, small, fc_proj, fc_bias, *out)


def per_device(
    sizes,
    inputs,
    doc_ids,
    cotangent,
    ln1_gain,
    ln1_shift,
    w_qkv,
    b_query,
    b_value,
    w_attn_out,
    b_attn_out,
    ln2_gain,
    ln2_shift,
    w_fc,
    b_fc,
    w_mlp_out,
    b_mlp_out,
):
    order_one, order_two = step_orders(sizes)
    tokens = inputs[0]
    grad_out = cotangent[0]
    group_docs = doc_ids[0]
    tok_count, width = tokens.shape
    dim = width // HEADS
    seq = sizes["seq"]
    far = seq // 2
    heads = HEADS // far
    rows = heads * dim
    position = lax.axis_index("seq")
    far_pos, near_pos = position // 2, position % 2

    shard_rows = w_qkv.shape[0]
    vectors = [ln1_gain, ln1_shift, b_query, b_value, b_attn_out, ln2_gain, ln2_shift, b_mlp_out]
    fc_rows = b_fc.shape[0] // shard_rows
    vectors += [b_fc[n * shard_rows : (n + 1) * shard_rows] for n in range(fc_rows)]
    zero = jnp.zeros((), bf16)
    small = sum(
        lax.pad(v[None], zero, ((n, len(vectors) - 1 - n, 0), (0, 0, 0)))
        for n, v in enumerate(vectors)
    ).T
    small_count = small.shape[1]
    small = jnp.pad(small, ((0, 0), (0, LANES - small_count)))
    half = w_qkv.shape[1] // 2

    qkv_one = gather(w_qkv[:, :half], order_one, sizes)
    qkv_two = gather(jnp.concatenate([w_qkv[:, half:], small], axis=1), order_two, sizes)
    fc_proj_full = gather(jnp.concatenate([w_fc, w_attn_out], axis=1), order_one, sizes)
    out_aligned = w_mlp_out.shape[0] % 32 == 0
    out_full = gather(w_mlp_out, order_two, sizes, join=not out_aligned)
    if not out_aligned:
        out_full = (out_full,)

    fc_bias = qkv_two[:, half + 8 : half + small_count].astype(f32)
    fc_bias = fc_bias.reshape(-1, shard_rows, fc_rows).swapaxes(1, 2).reshape(1, -1)

    block_docs = group_docs[::tok_count]
    own_blocks = 2 * jnp.arange(far, dtype=jnp.int32) + near_pos
    own_docs = jnp.take(block_docs, own_blocks)
    first_blocks = jnp.sum(
        (block_docs[None, :] < own_docs[:, None]).astype(jnp.int32), axis=1, dtype=jnp.int32
    )
    core_bit = own_bit(bits_of(sizes)[-1])
    where = jnp.concatenate(
        [jnp.stack([far_pos, near_pos]), first_blocks, jnp.stack([core_bit])]
    ).astype(jnp.int32)

    def shift_far(value, shift):
        return lax.ppermute(
            value, "seq", [(i, (i + 2 * shift) % seq) for i in range(seq)]
        )

    def spread(slots):
        out = [slots[0]]
        for s in range(1, far):
            out.append(shift_far(slots[s], s))
        return out

    def collect(slots):
        out = [slots[0]]
        for s in range(1, far):
            out.append(shift_far(slots[s], far - s))
        return out

    def in_order(slots):
        stacked = jnp.stack(slots)
        return jnp.concatenate(
            [
                lax.dynamic_index_in_dim(stacked, lax.rem(g - far_pos + far, far), 0, keepdims=False)
                for g in range(far)
            ]
        )

    def to_pair(value):
        return lax.ppermute(value, "seq", [(i, i ^ 1) for i in range(seq)])

    attn_in, small, *slots = project(where, tokens, qkv_one, qkv_two, rows, far)
    key_slots = spread(slots[far:])
    query_slots = spread(slots[:far])
    pair_slots = []
    for value in key_slots:
        pair_slots.append(to_pair(value))
    own, pair, head_out, lse, *out_slots = attend(
        where, query_slots, key_slots, pair_slots, heads, dim
    )
    out_slots = collect(out_slots)
    (
        result,
        attended_t,
        mlp_in,
        resid_bf,
        grad_resid,
        middle_sums,
        hidden_bf,
        hidden_grad_bf,
        g_fc_b,
        *grad_slots,
    ) = middle(
        where, tokens, grad_out, out_slots, fc_proj_full, small, out_full, fc_bias, rows
    )
    grad_slots = spread(grad_slots)
    grad_bf = grad_out.astype(bf16)
    sort_one, sort_two = (send_order(o, sizes, width) for o in (order_one, order_two))
    part = width // 2

    g_out_w = dot(hidden_bf, grad_bf, 0, 0).astype(bf16)
    g_out_w = scatter_sum(g_out_w, order_two, sizes)
    both_sorted = dot(jnp.concatenate([mlp_in, attn_in]), sort_one, 1, 0).astype(bf16)
    mlp_sorted, sorted_one = both_sorted[:tok_count], both_sorted[tok_count:]
    att_sorted = dot(sort_one, attended_t, 0, 0).astype(bf16)
    fc_cols = hidden_grad_bf.shape[1]

    def fc_proj(low, high):
        g_fc = dot(mlp_sorted[:, low:high], hidden_grad_bf, 0, 0).astype(bf16)
        g_proj = dot(att_sorted[low:high], resid_bf, 1, 0).astype(bf16)
        return jnp.concatenate([g_fc, g_proj], axis=1)

    g_fc_proj = scatter_sorted(fc_proj(0, part), fc_proj(part, width), order_one, sizes)

    *back_slots, own_back = attend_back(
        where, own, pair, head_out, lse, grad_slots, heads, dim
    )
    from_pair = []
    for n in range(far):
        from_pair.append(to_pair(back_slots[far + n]))
    query_grad = in_order(collect(back_slots[:far]))
    key_slots = [(own_back[s] + from_pair[s].astype(f32)).astype(bf16) for s in range(far)]
    key_slots = collect(key_slots)
    qkv_grad_t = jnp.concatenate(
        [
            query_grad,
            in_order([v[:rows] for v in key_slots]),
            in_order([v[rows:] for v in key_slots]),
        ],
        axis=0,
    )
    sorted_two = dot(attn_in, sort_two, 1, 0).astype(bf16)
    g_qkv_one = [
        dot(sorted_one[:, low : low + part], qkv_grad_t[:half], 0, 1).astype(bf16)
        for low in (0, part)
    ]
    g_qkv_one = scatter_sorted(*g_qkv_one, order_one, sizes)
    grad_first = dot(qkv_grad_t[:half], qkv_one, 0, 1) + dot(
        qkv_grad_t[half:], qkv_two[:, :half], 0, 1
    )
    g_query_b = jnp.sum(qkv_grad_t[:width].astype(f32), axis=1, keepdims=True)
    g_value_b = jnp.sum(qkv_grad_t[2 * width :].astype(f32), axis=1, keepdims=True)
    gain_one = small[0:1]
    late_tokens, grad_first = lax.optimization_barrier((tokens, grad_first))
    _, normal_one, inverse_one = layer_norm(late_tokens, gain_one, gain_one)
    g_gain_one = jnp.sum(grad_first * normal_one, axis=0)
    g_shift_one = jnp.sum(grad_first, axis=0)
    grad_input = grad_resid + norm_back(grad_first, normal_one, inverse_one, gain_one)

    row_sums = jnp.concatenate([g_gain_one[None], g_shift_one[None], middle_sums[:4]]).T
    sums = jnp.concatenate([row_sums, g_query_b, g_value_b, g_fc_b.reshape(width, -1)], axis=1)
    sums = jnp.pad(sums, ((0, 0), (0, LANES - sums.shape[1]))).astype(bf16)
    sums = dot(sort_two, sums, 0, 0).astype(bf16)

    def qkv_sums(low, high):
        g_two = dot(sorted_two[:, low:high], qkv_grad_t[half:], 0, 1).astype(bf16)
        return jnp.concatenate([g_two, sums[low:high]], axis=1)

    g_qkv_two = scatter_sorted(qkv_sums(0, part), qkv_sums(part, width), order_two, sizes)
    g_qkv_two, sums = g_qkv_two[:, :half], g_qkv_two[:, half:]
    return (
        result[None],
        grad_input[None],
        sums[:, 0],
        sums[:, 1],
        jnp.concatenate([g_qkv_one, g_qkv_two], axis=1),
        sums[:, 6],
        sums[:, 7],
        g_fc_proj[:, fc_cols:],
        sums[:, 2],
        sums[:, 3],
        sums[:, 4],
        g_fc_proj[:, :fc_cols],
        sums[:, 8:small_count].reshape(-1),
        g_out_w,
        sums[:, 5],
    )


def solution(mesh):
    vector, matrix = P(("seq", "dp")), P(("seq", "dp"), None)
    block = P("dp", "seq", None)
    in_specs = (
        block,
        P("dp", None),
        block,
        vector,
        vector,
        matrix,
        vector,
        vector,
        matrix,
        vector,
        vector,
        vector,
        matrix,
        vector,
        matrix,
        vector,
    )
    out_specs = (
        block,
        block,
        vector,
        vector,
        matrix,
        vector,
        vector,
        matrix,
        vector,
        vector,
        vector,
        matrix,
        vector,
        matrix,
        vector,
    )

    def body(*args):
        return per_device(dict(mesh.shape), *args)

    return jax.shard_map(body, mesh=mesh, in_specs=in_specs, out_specs=out_specs, check_vma=False)
```

```python
import functools

import jax
import jax.numpy as jnp
from jax import lax
from jax.experimental import pallas as pl
from jax.experimental.pallas import tpu as pltpu
from jax.sharding import PartitionSpec as P


HEADS = 12
LANES = 128

norm_eps = 1e-05
gelu_root = 0.7978845608028654
gelu_cube = 0.044715
score_scale = 0.125
hidden_score = -1e30


bf16 = jnp.bfloat16
f32 = jnp.float32


def layer_norm(values, gain, shift):
    average = jnp.mean(values, axis=-1, keepdims=True)
    centred = values - average
    variance = jnp.mean(centred * centred, axis=-1, keepdims=True)
    inverse = lax.rsqrt(variance + norm_eps)
    normed = centred * inverse
    return (normed * gain + shift, normed, inverse)


def norm_back(grad_out, normed, inverse, gain):
    scaled = grad_out * gain
    first = jnp.mean(scaled, axis=-1, keepdims=True)
    second = jnp.mean(scaled * normed, axis=-1, keepdims=True)
    return inverse * (scaled - first - normed * second)


def gelu_pair(values):
    inner = gelu_root * (values + gelu_cube * values * values * values)
    tangent = jnp.tanh(inner)
    output = 0.5 * values * (1.0 + tangent)
    slope = 0.5 * (1.0 + tangent) + 0.5 * values * (1.0 - tangent * tangent) * gelu_root * (
        1.0 + 3.0 * gelu_cube * values * values
    )
    return (output, slope)


def dot(left, right, left_dim, right_dim):
    return lax.dot_general(
        left, right, (((left_dim,), (right_dim,)), ((), ())), preferred_element_type=f32
    )


def bits_of(sizes):
    out = []
    for axis in ("seq", "dp"):
        bit = sizes[axis] // 2
        while bit >= 1:
            out.append((axis, bit))
            bit //= 2
    return out


def step_orders(sizes):
    order = bits_of(sizes)
    seq_bits = [s for s in order if s[0] == "seq"]
    dp_bits = [s for s in order if s[0] == "dp"]
    far, near = seq_bits[:-1], seq_bits[-1:]
    side, core = dp_bits[:-1], dp_bits[-1:]
    return (far + near + side + core, far + side + near + core)


def own_bit(step):
    axis, bit = step
    return (lax.axis_index(axis) // bit) % 2


def exchange(value, step, sizes):
    axis, bit = step
    return lax.ppermute(value, axis, [(i, i ^ bit) for i in range(sizes[axis])])


def gather(shard, steps, sizes, join=True):
    place = {step: n for n, step in enumerate(bits_of(sizes))}
    have, value = [], shard
    for n, step in enumerate(steps):
        if n == len(steps) - 1 and not join:
            value = lax.optimization_barrier(value.reshape((-1,) + shard.shape))
        other = exchange(value, step, sizes)
        if n == len(steps) - 1 and not join:
            return (value, other)
        at = sum(1 for m in have if m < place[step])
        have.append(place[step])
        mine, other = jnp.expand_dims(value, at), jnp.expand_dims(other, at)
        shape = mine.shape[:at] + (2,) + mine.shape[at + 1 :]
        side = lax.broadcasted_iota(jnp.int32, shape, at)
        value = jnp.where(side == own_bit(step), mine, other)
    return value.reshape(-1, shard.shape[1])


def scatter_sum(full, steps, sizes):
    order = bits_of(sizes)
    count = 2 ** len(order)
    value = full.reshape((2,) * len(order) + (full.shape[0] // count,) + full.shape[1:])
    left = list(order)
    for step in reversed(steps):
        at = left.index(step)
        left.remove(step)
        low = lax.index_in_dim(value, 0, at, keepdims=False)
        high = lax.index_in_dim(value, 1, at, keepdims=False)
        upper = own_bit(step) == 1
        got = exchange(jnp.where(upper, low, high), step, sizes)
        value = jnp.where(upper, high, low).astype(f32) + got.astype(f32)
        if left:
            value = value.astype(bf16)
    return value


def scatter_sorted(send, keep, steps, sizes):
    for n, step in enumerate(reversed(steps)):
        got = exchange(send, step, sizes)
        total = keep.astype(f32) + got.astype(f32)
        if n < len(steps) - 1:
            rows = total.shape[0] // 2
            send, keep = total[:rows].astype(bf16), total[rows:].astype(bf16)
    return total


def send_order(steps, sizes, width):
    order = bits_of(sizes)
    count = len(order)
    rows = width // 2**count
    column = lax.broadcasted_iota(jnp.int32, (1, width), 1)
    at, inside = column // rows, column % rows
    owner = lax.axis_index("seq") * sizes["dp"] + lax.axis_index("dp")
    for n, step in enumerate(reversed(steps)):
        other = 1 - (at >> (count - 1 - n)) % 2
        owner = owner ^ (other << (count - 1 - order.index(step)))
    row = lax.broadcasted_iota(jnp.int32, (width, width), 0)
    return (row == owner * rows + inside).astype(bf16)


def block_slot(far_pos, index, far):
    return lax.rem(far_pos - index + far, far)


def triangle(size):
    key_pos = lax.broadcasted_iota(jnp.int32, (size, size), 0)
    query_pos = lax.broadcasted_iota(jnp.int32, (size, size), 1)
    return jnp.where(key_pos <= query_pos, 0.0, hidden_score)


def forward_kernel(heads, dim, far, where_ref, *refs):
    query_refs, key_refs, pair_refs = refs[:far], refs[far : 2 * far], refs[2 * far : 3 * far]
    own_ref, pair_ref, out_ref, lse_ref = refs[3 * far : 3 * far + 4]
    slot_refs, tri_ref = refs[3 * far + 4 : 4 * far + 4], refs[4 * far + 4]
    far_pos, near_pos = where_ref[0], where_ref[1]
    rows = heads * dim
    for s in range(far):
        own_ref[s, :rows, :] = query_refs[s][...]
        own_ref[s, rows:, :] = key_refs[s][...]
        pair_ref[s] = pair_refs[s][...]
    tri_ref[0] = jnp.zeros(tri_ref.shape[1:], f32)
    tri_ref[1] = triangle(tri_ref.shape[1])

    def head_rows(part, head):
        return pl.ds(part * rows + head * dim, dim)

    def query_block(j, _):
        first = where_ref[2 + j]
        slot_j = block_slot(far_pos, j, far)
        queries = [
            own_ref[slot_j, head_rows(0, h), :] * jnp.asarray(score_scale, bf16)
            for h in range(heads)
        ]

        def tiles(i, state):
            slot_i = block_slot(far_pos, i, far)
            own_at, pair_at = 2 * i + near_pos, 2 * i + 1 - near_pos
            own_bias = jnp.where(own_at >= first, 0.0, hidden_score)
            diagonal = (i == j).astype(jnp.int32)
            pair_seen = (pair_at >= first) & (pair_at < 2 * j + near_pos)
            pair_bias = jnp.where(pair_seen, 0.0, hidden_score)
            out = []
            for h in range(heads):
                top, total, acc = state[h]
                own = dot(own_ref[slot_i, head_rows(1, h), :], queries[h], 0, 0)
                own = own + tri_ref[diagonal] + own_bias
                pair = dot(pair_ref[slot_i, head_rows(0, h), :], queries[h], 0, 0) + pair_bias
                new_top = jnp.maximum(top, jnp.max(jnp.maximum(own, pair), axis=0, keepdims=True))
                own = jnp.exp(own - new_top)
                pair = jnp.exp(pair - new_top)
                shrink = jnp.exp(top - new_top)
                total = total * shrink + jnp.sum(own + pair, axis=0, keepdims=True)
                acc = (
                    acc * shrink
                    + dot(own_ref[slot_i, head_rows(2, h), :], own.astype(bf16), 1, 0)
                    + dot(pair_ref[slot_i, head_rows(1, h), :], pair.astype(bf16), 1, 0)
                )
                out.append((new_top, total, acc))
            return tuple(out)

        size = own_ref.shape[2]
        state = tuple(
            (
                jnp.full((1, size), hidden_score, f32),
                jnp.zeros((1, size), f32),
                jnp.zeros((dim, size), f32),
            )
            for _ in range(heads)
        )
        state = lax.fori_loop(first // 2, j + 1, tiles, state)
        for h in range(heads):
            top, total, acc = state[h]
            done = acc / total
            out_ref[slot_j, pl.ds(h * dim, dim), :] = done
            lse_ref[slot_j, pl.ds(h, 1), :] = top + jnp.log(total)
        return 0

    lax.fori_loop(0, far, query_block, 0)
    for s in range(far):
        slot_refs[s][...] = out_ref[s].astype(bf16)


def backward_kernel(heads, dim, far, where_ref, own_ref, pair_ref, out_ref, lse_ref, *refs):
    grad_refs, query_refs, pair_grad_refs = refs[:far], refs[far : 2 * far], refs[2 * far : 3 * far]
    own_grad_ref, grad_ref, query_ref, tri_ref, acc_ref = refs[3 * far :]
    far_pos, near_pos = where_ref[0], where_ref[1]
    rows = heads * dim
    for s in range(far):
        grad_ref[s] = grad_refs[s][...]
    tri_ref[0] = jnp.zeros(tri_ref.shape[1:], f32)
    tri_ref[1] = triangle(tri_ref.shape[1])
    own_grad_ref[...] = jnp.zeros(own_grad_ref.shape, f32)
    acc_ref[...] = jnp.zeros(acc_ref.shape, f32)

    def head_rows(part, head):
        return pl.ds(part * rows + head * dim, dim)

    def query_block(j, _):
        first = where_ref[2 + j]
        slot_j = block_slot(far_pos, j, far)
        queries = [
            own_ref[slot_j, head_rows(0, h), :] * jnp.asarray(score_scale, bf16)
            for h in range(heads)
        ]
        grads = [grad_ref[slot_j, head_rows(0, h), :] for h in range(heads)]
        deltas = [
            jnp.sum(grads[h].astype(f32) * out_ref[slot_j, head_rows(0, h), :], axis=0, keepdims=True)
            for h in range(heads)
        ]
        lses = [lse_ref[slot_j, pl.ds(h, 1), :] for h in range(heads)]

        def tile(h, keys, vals, bias, mask, into, slot_i):
            scores = dot(keys, queries[h], 0, 0)
            if mask is not None:
                scores = scores + tri_ref[mask]
            prob = jnp.exp(scores - (lses[h] - bias))
            grad_prob = dot(vals, grads[h], 0, 0)
            grad_score = (prob * (grad_prob - deltas[h])).astype(bf16)
            into[slot_i, head_rows(0, h), :] += dot(queries[h], grad_score, 1, 1)
            into[slot_i, head_rows(1, h), :] += dot(grads[h], prob.astype(bf16), 1, 1)
            return dot(keys, grad_score, 1, 0)

        def tiles(i, state):
            slot_i = block_slot(far_pos, i, far)
            own_at, pair_at = 2 * i + near_pos, 2 * i + 1 - near_pos
            own_bias = jnp.where(own_at >= first, 0.0, hidden_score)
            diagonal = (i == j).astype(jnp.int32)
            pair_seen = (pair_at >= first) & (pair_at < 2 * j + near_pos)
            pair_bias = jnp.where(pair_seen, 0.0, hidden_score)
            out = []
            for h in range(heads):
                own = tile(
                    h,
                    own_ref[slot_i, head_rows(1, h), :],
                    own_ref[slot_i, head_rows(2, h), :],
                    own_bias,
                    diagonal,
                    own_grad_ref,
                    slot_i,
                )
                pair = tile(
                    h,
                    pair_ref[slot_i, head_rows(0, h), :],
                    pair_ref[slot_i, head_rows(1, h), :],
                    pair_bias,
                    None,
                    acc_ref,
                    slot_i,
                )
                out.append(state[h] + own + pair)
            return tuple(out)

        size = own_ref.shape[2]
        state = tuple(jnp.zeros((dim, size), f32) for _ in range(heads))
        state = lax.fori_loop(first // 2, j + 1, tiles, state)
        for h in range(heads):
            query_ref[slot_j, head_rows(0, h), :] = (state[h] * score_scale).astype(bf16)
        return 0

    lax.fori_loop(0, far, query_block, 0)
    for s in range(far):
        query_refs[s][...] = query_ref[s]
        pair_grad_refs[s][...] = acc_ref[s].astype(bf16)


def vmem():
    return pl.BlockSpec(memory_space=pltpu.VMEM)


def attend(where, queries, keys, pairs, heads, dim):
    far, size, rows = len(queries), queries[0].shape[1], heads * dim
    return pl.pallas_call(
        functools.partial(forward_kernel, heads, dim, far),
        name="attend",
        out_shape=(
            jax.ShapeDtypeStruct((far, 3 * rows, size), bf16),
            jax.ShapeDtypeStruct((far, 2 * rows, size), bf16),
            jax.ShapeDtypeStruct((far, rows, size), f32),
            jax.ShapeDtypeStruct((far, 8, size), f32),
        )
        + (jax.ShapeDtypeStruct((rows, size), bf16),) * far,
        in_specs=[pl.BlockSpec(memory_space=pltpu.SMEM)] + [vmem()] * (3 * far),
        out_specs=(vmem(),) * (4 + far),
        scratch_shapes=[pltpu.VMEM((2, size, size), f32)],
        cost_estimate=pl.CostEstimate(
            flops=16 * heads * 4 * dim * size * size,
            bytes_accessed=24 * far * rows * size,
            transcendentals=16 * heads * size * size,
        ),
    )(where, *queries, *keys, *pairs)


def attend_back(where, own, pair, out, lse, grads, heads, dim):
    far, size, rows = len(grads), own.shape[2], heads * dim
    return pl.pallas_call(
        functools.partial(backward_kernel, heads, dim, far),
        name="attend_back",
        out_shape=(jax.ShapeDtypeStruct((rows, size), bf16),) * far
        + (jax.ShapeDtypeStruct((2 * rows, size), bf16),) * far
        + (jax.ShapeDtypeStruct((far, 2 * rows, size), f32),),
        in_specs=[pl.BlockSpec(memory_space=pltpu.SMEM)] + [vmem()] * (4 + far),
        out_specs=(vmem(),) * (2 * far + 1),
        scratch_shapes=[
            pltpu.VMEM((far, rows, size), bf16),
            pltpu.VMEM((far, rows, size), bf16),
            pltpu.VMEM((2, size, size), f32),
            pltpu.VMEM((far, 2 * rows, size), f32),
        ],
        cost_estimate=pl.CostEstimate(
            flops=16 * heads * 10 * dim * size * size,
            bytes_accessed=32 * far * rows * size,
            transcendentals=16 * heads * size * size,
        ),
    )(where, own, pair, out, lse, *grads)


def project_kernel(rows, far, where_ref, tokens_ref, one_ref, two_ref, normed_ref, small_ref, *refs):
    query_refs, key_refs, all_ref = refs[:far], refs[far : 2 * far], refs[2 * far]
    width, half = tokens_ref.shape[1], one_ref.shape[1]
    columns = two_ref[:, half:].astype(f32)
    small = columns.T[: small_ref.shape[0]]
    small_ref[...] = small
    normed = layer_norm(tokens_ref[...], small[0:1], small[1:2])[0].astype(bf16)
    normed_ref[...] = normed
    one = dot(one_ref[...], normed, 0, 1)
    all_ref[:width, :] = (one[:width] + columns[:, 2:3]).astype(bf16)
    all_ref[width:half, :] = one[width:].astype(bf16)
    two = dot(two_ref[:, :half], normed, 0, 1)
    cut = 2 * width - half
    all_ref[half : 2 * width, :] = two[:cut].astype(bf16)
    all_ref[2 * width :, :] = (two[cut:] + columns[:, 3:4]).astype(bf16)
    for s in range(far):
        first = lax.rem(where_ref[0] + s, far) * rows
        for part, ref, at in ((0, query_refs[s], 0), (1, key_refs[s], 0), (2, key_refs[s], rows)):
            start = pl.multiple_of(part * width + first, rows)
            ref[pl.ds(at, rows), :] = all_ref[pl.ds(start, rows), :]


def project(where, tokens, one, two, rows, far):
    size, width = tokens.shape
    return pl.pallas_call(
        functools.partial(project_kernel, rows, far),
        name="project",
        out_shape=(
            jax.ShapeDtypeStruct((size, width), bf16),
            jax.ShapeDtypeStruct((8, width), f32),
        )
        + (jax.ShapeDtypeStruct((rows, size), bf16),) * far
        + (jax.ShapeDtypeStruct((2 * rows, size), bf16),) * far,
        in_specs=[pl.BlockSpec(memory_space=pltpu.SMEM)] + [vmem()] * 3,
        out_specs=(vmem(),) * (2 + 2 * far),
        scratch_shapes=[pltpu.VMEM((3 * width, size), bf16)],
        cost_estimate=pl.CostEstimate(
            flops=6 * size * width * width, bytes_accessed=12 * width * width, transcendentals=0
        ),
    )(where, tokens, one, two)


def middle_kernel(rows, far, pieces, where_ref, tokens_ref, cot_ref, *refs):
    slot_refs = refs[:far]
    proj_ref, small_ref, fc_ref, fc_bias_ref = refs[far : far + 4]
    out_refs = refs[far + 4 : far + 4 + pieces]
    refs = refs[far + 4 + pieces :]
    (result_ref, att_ref, mlp_ref, resid_ref, grad_resid_ref, sums_ref) = refs[:6]
    hidden_ref, hidden_grad_ref, fc_sum_ref = refs[6:9]
    grad_refs = refs[9 : 9 + far]
    normal_ref, inverse_ref, acc_ref, cot_bf_ref, back_ref, out_ref = refs[9 + far :]
    step = pl.program_id(0)

    @pl.when(step == 0)
    def _():
        for s in range(far):
            first = pl.multiple_of(lax.rem(where_ref[0] + s, far) * rows, rows)
            att_ref[pl.ds(first, rows), :] = slot_refs[s][...]
        resid = tokens_ref[...] + dot(att_ref[...], proj_ref[...], 0, 0) + small_ref[4:5]
        normed, normal, inverse = layer_norm(resid, small_ref[5:6], small_ref[6:7])
        mlp_ref[...] = normed.astype(bf16)
        normal_ref[...] = normal
        inverse_ref[...] = jnp.broadcast_to(inverse, inverse_ref.shape)
        result_ref[...] = resid + small_ref[7:8]
        cot_bf_ref[...] = cot_ref[...].astype(bf16)
        acc_ref[...] = jnp.zeros(acc_ref.shape, f32)

    weight_in = fc_ref[...]
    if pieces == 1:
        weight_out = out_refs[0][...]
    else:
        count, piece = out_refs[0].shape[:2]
        for side, ref in enumerate(out_refs):
            core = (where_ref[2 + far] + side) % 2
            for n in range(count):
                start = pl.multiple_of((2 * n + core) * piece, 32)
                out_ref[pl.ds(start, piece), :] = ref[n]
        weight_out = out_ref[...]
    pre = dot(mlp_ref[...], weight_in, 1, 0) + fc_bias_ref[...]
    act, slope = gelu_pair(pre)
    hidden = act.astype(bf16)
    hidden_ref[...] = hidden
    result_ref[...] += dot(hidden, weight_out, 1, 0)
    grad = dot(cot_bf_ref[...], weight_out, 1, 1) * slope
    fc_sum_ref[...] = jnp.sum(grad, axis=0, keepdims=True)
    grad = grad.astype(bf16)
    hidden_grad_ref[...] = grad
    acc_ref[...] += dot(grad, weight_in, 1, 1)

    @pl.when(step == pl.num_programs(0) - 1)
    def _():
        normal, grad_mid, cot = normal_ref[...], acc_ref[...], cot_ref[...]
        back = norm_back(grad_mid, normal, inverse_ref[:, 0:1], small_ref[5:6])
        grad_resid = cot + back
        grad_resid_ref[...] = grad_resid
        resid_bf = grad_resid.astype(bf16)
        resid_ref[...] = resid_bf
        back_ref[...] = dot(proj_ref[...], resid_bf, 1, 1).astype(bf16)
        for s in range(far):
            first = pl.multiple_of(lax.rem(where_ref[0] + s, far) * rows, rows)
            grad_refs[s][...] = back_ref[pl.ds(first, rows), :]
        totals = (grad_resid, grad_mid * normal, grad_mid, cot)
        sums_ref[0:4, :] = jnp.concatenate(
            [jnp.sum(value, axis=0, keepdims=True) for value in totals], axis=0
        )
        sums_ref[4:8, :] = jnp.zeros((4, sums_ref.shape[1]), f32)


def middle(where, tokens, cot, slots, fc_proj, small, out, fc_bias, rows):
    far, (size, width), hidden = len(slots), tokens.shape, fc_bias.shape[1]
    cut = width
    steps = hidden // cut

    def whole(shape):
        return pl.BlockSpec(shape, lambda f: (0,) * len(shape))

    token_spec, rows_spec = whole((size, width)), whole((rows, size))
    hidden_spec = pl.BlockSpec((size, cut), lambda f: (0, f))
    bias_spec = pl.BlockSpec((1, cut), lambda f: (0, f))
    if len(out) == 1:
        out_specs = [pl.BlockSpec((cut, width), lambda f: (f, 0))]
    else:
        piece = out[0].shape[1]
        out_specs = [pl.BlockSpec((cut // piece // 2, piece, width), lambda f: (f, 0, 0))] * 2
    return pl.pallas_call(
        functools.partial(middle_kernel, rows, far, len(out)),
        name="middle",
        grid=(steps,),
        out_shape=(
            jax.ShapeDtypeStruct((size, width), f32),
            jax.ShapeDtypeStruct((width, size), bf16),
            jax.ShapeDtypeStruct((size, width), bf16),
            jax.ShapeDtypeStruct((size, width), bf16),
            jax.ShapeDtypeStruct((size, width), f32),
            jax.ShapeDtypeStruct((8, width), f32),
            jax.ShapeDtypeStruct((size, hidden), bf16),
            jax.ShapeDtypeStruct((size, hidden), bf16),
            jax.ShapeDtypeStruct((1, hidden), f32),
        )
        + (jax.ShapeDtypeStruct((rows, size), bf16),) * far,
        in_specs=[pl.BlockSpec(memory_space=pltpu.SMEM), token_spec, token_spec]
        + [rows_spec] * far
        + [
            pl.BlockSpec((width, width), lambda f: (0, hidden // width)),
            whole((8, width)),
            pl.BlockSpec((width, cut), lambda f: (0, f)),
            bias_spec,
        ]
        + out_specs,
        out_specs=(
            token_spec,
            whole((width, size)),
            token_spec,
            token_spec,
            token_spec,
            whole((8, width)),
            hidden_spec,
            hidden_spec,
            bias_spec,
        )
        + (rows_spec,) * far,
        scratch_shapes=[
            pltpu.VMEM((size, width), f32),
            pltpu.VMEM((size, LANES), f32),
            pltpu.VMEM((size, width), f32),
            pltpu.VMEM((size, width), bf16),
            pltpu.VMEM((width, size), bf16),
            pltpu.VMEM((cut, width), bf16),
        ],
        cost_estimate=pl.CostEstimate(
            flops=8 * size * width * hidden + 4 * size * width * width,
            bytes_accessed=4 * width * hidden + 4 * size * hidden + 24 * size * width,
            transcendentals=size * hidden,
        ),
    )(where, tokens, cot, *slots, fc_proj, small, fc_proj, fc_bias, *out)


def per_device(
    sizes,
    inputs,
    doc_ids,
    cotangent,
    ln1_gain,
    ln1_shift,
    w_qkv,
    b_query,
    b_value,
    w_attn_out,
    b_attn_out,
    ln2_gain,
    ln2_shift,
    w_fc,
    b_fc,
    w_mlp_out,
    b_mlp_out,
):
    order_one, order_two = step_orders(sizes)
    tokens = inputs[0]
    grad_out = cotangent[0]
    group_docs = doc_ids[0]
    tok_count, width = tokens.shape
    dim = width // HEADS
    seq = sizes["seq"]
    far = seq // 2
    heads = HEADS // far
    rows = heads * dim
    position = lax.axis_index("seq")
    far_pos, near_pos = position // 2, position % 2

    shard_rows = w_qkv.shape[0]
    vectors = [ln1_gain, ln1_shift, b_query, b_value, b_attn_out, ln2_gain, ln2_shift, b_mlp_out]
    fc_rows = b_fc.shape[0] // shard_rows
    vectors += [b_fc[n * shard_rows : (n + 1) * shard_rows] for n in range(fc_rows)]
    zero = jnp.zeros((), bf16)
    small = sum(
        lax.pad(v[None], zero, ((n, len(vectors) - 1 - n, 0), (0, 0, 0)))
        for n, v in enumerate(vectors)
    ).T
    small_count = small.shape[1]
    small = jnp.pad(small, ((0, 0), (0, LANES - small_count)))
    half = w_qkv.shape[1] // 2

    qkv_one = gather(w_qkv[:, :half], order_one, sizes)
    qkv_two = gather(jnp.concatenate([w_qkv[:, half:], small], axis=1), order_two, sizes)
    fc_proj_full = lax.optimization_barrier(
        gather(jnp.concatenate([w_fc, w_attn_out], axis=1), order_one, sizes)
    )
    out_aligned = w_mlp_out.shape[0] % 32 == 0
    out_full = gather(w_mlp_out, order_two, sizes, join=not out_aligned)
    if not out_aligned:
        out_full = (out_full,)

    fc_bias = qkv_two[:, half + 8 : half + small_count].astype(f32)
    fc_bias = fc_bias.reshape(-1, shard_rows, fc_rows).swapaxes(1, 2).reshape(1, -1)

    block_docs = group_docs[::tok_count]
    own_blocks = 2 * jnp.arange(far, dtype=jnp.int32) + near_pos
    own_docs = jnp.take(block_docs, own_blocks)
    first_blocks = jnp.sum(
        (block_docs[None, :] < own_docs[:, None]).astype(jnp.int32), axis=1, dtype=jnp.int32
    )
    core_bit = own_bit(bits_of(sizes)[-1])
    where = jnp.concatenate(
        [jnp.stack([far_pos, near_pos]), first_blocks, jnp.stack([core_bit])]
    ).astype(jnp.int32)

    def shift_far(value, shift):
        return lax.ppermute(
            value, "seq", [(i, (i + 2 * shift) % seq) for i in range(seq)]
        )

    def spread(slots):
        out = [slots[0]]
        for s in range(1, far):
            out.append(shift_far(slots[s], s))
        return out

    def collect(slots):
        out = [slots[0]]
        for s in range(1, far):
            out.append(shift_far(slots[s], far - s))
        return out

    def in_order(slots):
        stacked = jnp.stack(slots)
        return jnp.concatenate(
            [
                lax.dynamic_index_in_dim(stacked, lax.rem(g - far_pos + far, far), 0, keepdims=False)
                for g in range(far)
            ]
        )

    def to_pair(value):
        return lax.ppermute(value, "seq", [(i, i ^ 1) for i in range(seq)])

    attn_in, small, *slots = project(where, tokens, qkv_one, qkv_two, rows, far)
    key_slots = spread(slots[far:])
    query_slots = spread(slots[:far])
    pair_slots = []
    for value in key_slots:
        pair_slots.append(to_pair(value))
    own, pair, head_out, lse, *out_slots = attend(
        where, query_slots, key_slots, pair_slots, heads, dim
    )
    out_slots = collect(out_slots)
    (
        result,
        attended_t,
        mlp_in,
        resid_bf,
        grad_resid,
        middle_sums,
        hidden_bf,
        hidden_grad_bf,
        g_fc_b,
        *grad_slots,
    ) = middle(
        where, tokens, grad_out, out_slots, fc_proj_full, small, out_full, fc_bias, rows
    )
    grad_slots = spread(grad_slots)
    grad_bf = grad_out.astype(bf16)
    sort_one, sort_two = (send_order(o, sizes, width) for o in (order_one, order_two))
    part = width // 2

    g_out_w = dot(hidden_bf, grad_bf, 0, 0).astype(bf16)
    g_out_w = scatter_sum(g_out_w, order_two, sizes)
    both_sorted = dot(jnp.concatenate([mlp_in, attn_in]), sort_one, 1, 0).astype(bf16)
    mlp_sorted, sorted_one = both_sorted[:tok_count], both_sorted[tok_count:]
    att_sorted = dot(sort_one, attended_t, 0, 0).astype(bf16)
    fc_cols = hidden_grad_bf.shape[1]

    def fc_proj(low, high):
        g_fc = dot(mlp_sorted[:, low:high], hidden_grad_bf, 0, 0).astype(bf16)
        g_proj = dot(att_sorted[low:high], resid_bf, 1, 0).astype(bf16)
        return jnp.concatenate([g_fc, g_proj], axis=1)

    g_fc_proj = scatter_sorted(fc_proj(0, part), fc_proj(part, width), order_one, sizes)

    *back_slots, own_back = attend_back(
        where, own, pair, head_out, lse, grad_slots, heads, dim
    )
    from_pair = []
    for n in range(far):
        from_pair.append(to_pair(back_slots[far + n]))
    query_grad = in_order(collect(back_slots[:far]))
    key_slots = [(own_back[s] + from_pair[s].astype(f32)).astype(bf16) for s in range(far)]
    key_slots = collect(key_slots)
    qkv_grad_t = jnp.concatenate(
        [
            query_grad,
            in_order([v[:rows] for v in key_slots]),
            in_order([v[rows:] for v in key_slots]),
        ],
        axis=0,
    )
    late_attn, _ = lax.optimization_barrier((attn_in, back_slots[0]))
    sorted_two = dot(late_attn, sort_two, 1, 0).astype(bf16)
    g_qkv_one = [
        dot(sorted_one[:, low : low + part], qkv_grad_t[:half], 0, 1).astype(bf16)
        for low in (0, part)
    ]
    g_qkv_one = scatter_sorted(*g_qkv_one, order_one, sizes)
    grad_first = dot(qkv_grad_t[:half], qkv_one, 0, 1) + dot(
        qkv_grad_t[half:], qkv_two[:, :half], 0, 1
    )
    g_query_b = jnp.sum(qkv_grad_t[:width].astype(f32), axis=1, keepdims=True)
    g_value_b = jnp.sum(qkv_grad_t[2 * width :].astype(f32), axis=1, keepdims=True)
    gain_one = small[0:1]
    late_tokens, grad_first = lax.optimization_barrier((tokens, grad_first))
    _, normal_one, inverse_one = layer_norm(late_tokens, gain_one, gain_one)
    g_gain_one = jnp.sum(grad_first * normal_one, axis=0)
    g_shift_one = jnp.sum(grad_first, axis=0)
    grad_input = grad_resid + norm_back(grad_first, normal_one, inverse_one, gain_one)

    row_sums = jnp.concatenate([g_gain_one[None], g_shift_one[None], middle_sums[:4]]).T
    sums = jnp.concatenate([row_sums, g_query_b, g_value_b, g_fc_b.reshape(width, -1)], axis=1)
    sums = jnp.pad(sums, ((0, 0), (0, LANES - sums.shape[1]))).astype(bf16)
    sums = dot(sort_two, sums, 0, 0).astype(bf16)

    def qkv_sums(low, high):
        g_two = dot(sorted_two[:, low:high], qkv_grad_t[half:], 0, 1).astype(bf16)
        return jnp.concatenate([g_two, sums[low:high]], axis=1)

    g_qkv_two = scatter_sorted(qkv_sums(0, part), qkv_sums(part, width), order_two, sizes)
    g_qkv_two, sums = g_qkv_two[:, :half], g_qkv_two[:, half:]
    return (
        result[None],
        grad_input[None],
        sums[:, 0],
        sums[:, 1],
        jnp.concatenate([g_qkv_one, g_qkv_two], axis=1),
        sums[:, 6],
        sums[:, 7],
        g_fc_proj[:, fc_cols:],
        sums[:, 2],
        sums[:, 3],
        sums[:, 4],
        g_fc_proj[:, :fc_cols],
        sums[:, 8:small_count].reshape(-1),
        g_out_w,
        sums[:, 5],
    )


def solution(mesh):
    vector, matrix = P(("seq", "dp")), P(("seq", "dp"), None)
    block = P("dp", "seq", None)
    in_specs = (
        block,
        P("dp", None),
        block,
        vector,
        vector,
        matrix,
        vector,
        vector,
        matrix,
        vector,
        vector,
        vector,
        matrix,
        vector,
        matrix,
        vector,
    )
    out_specs = (
        block,
        block,
        vector,
        vector,
        matrix,
        vector,
        vector,
        matrix,
        vector,
        vector,
        vector,
        matrix,
        vector,
        matrix,
        vector,
    )

    def body(*args):
        return per_device(dict(mesh.shape), *args)

    return jax.shard_map(body, mesh=mesh, in_specs=in_specs, out_specs=out_specs, check_vma=False)
```
